32 devices in a mesh: visit: 8 (over y, x, core), sky: 4 (over z).
Axes of the slice: x: 2, y: 2, z: 4, core: 2. Of those that a mesh axis runs over, the one named last changes fastest.
Arguments:
- science: float32 [8, 16, 128, 128], P('visit', 'sky'), may hold values from -6 to 6
- coef_first: float32 [8, 16, 3, 49], P('visit', 'sky'), may hold values from -4 to 4
- coef_second: float32 [8, 16, 3, 49], P('visit', 'sky'), may hold values from -4 to 4
- weight: float32 [8, 16], P('visit', 'sky'), may hold values from 0.3 to 3
- slot_tile: int32 [8, 16], P('visit', 'sky'), may hold values from 0 to 3, as said below
- offsets: int32 [8, 16, 2], P('visit', 'sky'), may hold values from 0 to 128
- counts: int32 [8, 4], P('visit', 'sky'), may hold values from 3 to 4, as said below
- tile_place: int32 [4], replicated, may hold values from 0 to 3, as said below
Outputs:
- template: float32 [4, 256, 256], P('sky')
- difference: float32 [8, 16, 128, 128], P('visit', 'sky')
The draws below stay inside these ranges and needn't reach their ends.
Inputs may be any that keep to these rules, and one draw needn't show every extreme that they name: `slot_tile`: among the usable slots of one device's list at most 2 name tiles of one owner; in every visit the tile of some owner gets exactly 2 usable slots from every device of the sky axis. A permutation: tile t is owned by the device of sky index tile_place[t]. The first counts[v, s] slots of a device's list are usable; in every visit some device has all 4 usable.
All inputs are finite; a program needn't handle non-finite values.
Results may differ from the reference program's by a relative error of at most 0.00011.
Values sent between devices are 32-bit elements; how exact they have to be, the bound alone decides.
No kernel may reach another device: no remote copies, remote signals or barrier semaphores. Data moves between devices by JAX's collectives and lax.ppermute only.
A program may use at most 64 MiB of HBM per device.

```python
import math
import jax
import jax.numpy as jnp
from jax import lax

BLOCK = 128
TILE = 256
TAPS = 21
PROFILES = 7
SLOTS = 4
BASIS = 49
VISITS = 8
TILES = 4
LIST_SLOTS = 16
CAPACITY = 2


def routing(key):
    place = jax.random.permutation(jax.random.fold_in(key, 11), TILES).astype(jnp.int32)
    inverse = jnp.argsort(place, stable=True).astype(jnp.int32)
    tile_pairings = TILES * CAPACITY
    busiest_tile = jax.random.randint(jax.random.fold_in(key, 12), (VISITS, 1, 1), 0, TILES)
    kernel_driver = (busiest_tile + 1 + jax.random.randint(jax.random.fold_in(key, 13), (VISITS, 1, 1), 0, TILES - 1)) % TILES
    rank_positions = jax.random.randint(jax.random.fold_in(key, 14), (VISITS, TILES, tile_pairings), 0, 4096)
    pairing_holder = jnp.arange(tile_pairings, dtype=jnp.int32) // CAPACITY
    extra_credit = jnp.where(pairing_holder[None, None, :] == busiest_tile, 8 * 4096, 0) + jnp.where(pairing_holder[None, None, :] == kernel_driver, 2048, 0)
    tile_scores = (rank_positions + extra_credit) * tile_pairings + jnp.arange(tile_pairings, dtype=jnp.int32)[None, None, :]
    ordering = jnp.argsort(-tile_scores, axis=-1, stable=True)[:, :, :SLOTS]
    chosen = pairing_holder[ordering]
    tiles_named = jnp.take(inverse, chosen).reshape(VISITS, TILES * SLOTS)
    return (place, tiles_named.astype(jnp.int32))


def draw_slot_tile(key, part):
    return routing(key)[1]


def draw_tile_place(key, part):
    return routing(key)[0]


def draw_counts(key, part):
    lowest = SLOTS - 3 * SLOTS // 8
    drawn = jax.random.randint(jax.random.fold_in(key, 21), (VISITS, TILES), lowest, SLOTS + 1)
    return drawn.at[:, 0].set(SLOTS).astype(jnp.int32)


def set_ends(entries, rng, smallest, high):
    spot = [jax.random.randint(jax.random.fold_in(rng, axis), (), 0, length) for axis, length in enumerate(entries.shape)]
    longest = entries.shape.index(max(entries.shape))
    beside = spot[:longest] + [(spot[longest] + 1) % entries.shape[longest]] + spot[longest + 1:]
    return entries.at[tuple(spot)].set(smallest).at[tuple(beside)].set(high)


def levels(rng, extent, shards, smallest, high):
    def one(position, parts):
        steps = jax.random.uniform(jax.random.fold_in(jax.random.fold_in(rng, 6), position), (parts,), jnp.float32, smallest / len(shards), high / len(shards))
        return jnp.repeat(jnp.exp(steps), extent[position] // parts).reshape((-1,) + (1,) * (len(extent) - position - 1))

    gain = one(*shards[0])
    for cut in shards[1:]:
        gain = gain * one(*cut)
    return gain


def normal_values(key, shape, scale, most, pieces=(), kind=jnp.bfloat16):
    result = jax.random.normal(key, shape, jnp.float32) * scale
    if len(pieces) > 0:
        result = levels(key, shape, pieces, -0.22, 0.18) * result
    return jnp.clip(result, min=-most, max=most).astype(kind)


def setup_inputs(seed: int = 0) -> dict:
    streams_of = jax.random.split(jax.random.key(seed), 9)
    science = normal_values(streams_of[0], (VISITS, LIST_SLOTS, BLOCK, BLOCK), 1.0, 6.0, ((0, 8), (1, 4)), jnp.float32)
    coef_first = normal_values(streams_of[1], (VISITS, LIST_SLOTS, 3, BASIS), 0.3, 4.0, ((0, 8), (1, 4)), jnp.float32)
    coef_second = normal_values(streams_of[2], (VISITS, LIST_SLOTS, 3, BASIS), 0.3, 4.0, ((0, 8), (1, 4)), jnp.float32)
    weight = jnp.clip(jnp.exp(math.log(3.0) - 2.3025851 * jax.random.uniform(streams_of[3], (VISITS, LIST_SLOTS), jnp.float32) ** levels(streams_of[3], (VISITS, LIST_SLOTS), ((0, 8), (1, 4)), -0.2, 0.2)), 0.3, 3.0)
    slot_tile = draw_slot_tile(jax.random.fold_in(streams_of[8], 71), 0)
    offsets = set_ends(jax.random.randint(streams_of[5], (VISITS, LIST_SLOTS, 2), 0, TILE - BLOCK + 1), jax.random.fold_in(streams_of[5], 1), 0, TILE - BLOCK).astype(jnp.int32)
    counts = draw_counts(jax.random.fold_in(streams_of[8], 71), 0)
    tile_place = draw_tile_place(jax.random.fold_in(streams_of[8], 71), 0)
    return {"science": science, "coef_first": coef_first, "coef_second": coef_second, "weight": weight, "slot_tile": slot_tile, "offsets": offsets, "counts": counts, "tile_place": tile_place}


WIDTHS = (1.0, 1.0, 1.0, 2.5, 2.5, 2.5, 5.0)
POWERS = (0, 1, 2, 0, 1, 2, 0)
PRECISE = lax.Precision.HIGHEST

def profile_filters(side):
    reach = (TAPS - 1) // 2
    places = jnp.arange(side).astype(jnp.float32)
    spacing = places[None, :] - places[:, None]
    support = jnp.arange(TAPS).astype(jnp.float32) - reach
    stacked = []
    for number in range(PROFILES):
        sample = support ** POWERS[number] * jnp.exp(-support * support / (2.0 * WIDTHS[number] ** 2))
        norming = jnp.sqrt(jnp.sum(sample * sample))
        values = spacing ** POWERS[number] * jnp.exp(-spacing * spacing / (2.0 * WIDTHS[number] ** 2))
        stacked.append(jnp.where(jnp.abs(spacing) <= reach, values / norming, 0.0))
    return jnp.stack(stacked)

def positions(side):
    places = jnp.arange(side).astype(jnp.float32)
    return (2.0 * places - (side - 1)) / (side - 1)

def kernel_pass(block, coeffs, filters, spread):
    across_x = jnp.einsum('yw,ixw->iyx', block, filters, precision=PRECISE)
    layout = coeffs.reshape(3, PROFILES, PROFILES)
    plain = jnp.einsum('ij,jab->iab', layout[0], filters, precision=PRECISE)
    along = jnp.einsum('ij,jab->iab', layout[2], filters, precision=PRECISE) * spread[None, :, None]
    sideways = jnp.einsum('ij,jab->iab', layout[1], filters, precision=PRECISE)
    steady = jnp.einsum('iab,ibx->ax', plain + along, across_x, precision=PRECISE)
    varying = jnp.einsum('iab,ibx->ax', sideways, across_x, precision=PRECISE)
    return steady + varying * spread[None, :]

def reference(science, coef_first, coef_second, weight, slot_tile, offsets, counts, tile_place):
    filters = profile_filters(BLOCK)
    spread = positions(BLOCK)

    def convolve_visit(operands):
        return jax.vmap(lambda block, coeffs: kernel_pass(block, coeffs, filters, spread))(operands[0], operands[1])
    listed = jnp.arange(LIST_SLOTS) % SLOTS
    usable = listed[None, :] < jnp.repeat(counts, SLOTS, axis=1)
    owners = tile_place[slot_tile].astype(jnp.int32)
    convolved = lax.map(convolve_visit, (science, coef_first))
    weights_used = jnp.where(usable, weight, 0.0)

    def place_block(totals, item):
        weighted, coverage = totals
        block, block_weight, owner_index, corner = item
        anchor = (owner_index, corner[0], corner[1])
        region = lax.dynamic_slice(weighted, anchor, (1, BLOCK, BLOCK))
        weighted = lax.dynamic_update_slice(weighted, region + block_weight * block[None], anchor)
        region = lax.dynamic_slice(coverage, anchor, (1, BLOCK, BLOCK))
        coverage = lax.dynamic_update_slice(coverage, region + block_weight, anchor)
        return ((weighted, coverage), None)
    empty = jnp.zeros((TILES, TILE, TILE), jnp.float32)
    items = (convolved.reshape(-1, BLOCK, BLOCK), weights_used.reshape(-1), owners.reshape(-1), offsets.reshape(-1, 2).astype(jnp.int32))
    (weighted, coverage), unused = lax.scan(place_block, (empty, empty), items)
    template = weighted / (coverage + 1.0)

    def window(owner_index, corner):
        return lax.dynamic_slice(template, (owner_index, corner[0], corner[1]), (1, BLOCK, BLOCK))[0]
    cutout = jax.vmap(window)(items[2], items[3]).reshape(VISITS, LIST_SLOTS, BLOCK, BLOCK)
    matched = lax.map(convolve_visit, (cutout, coef_second))
    difference = jnp.where(usable[:, :, None, None], science - matched, 0.0)
    return (template, difference)
```

```python
import numpy as np
import jax
import jax.numpy as jnp
from jax import lax
from jax.experimental import pallas as pl
from jax.experimental.pallas import tpu as pltpu
from jax.sharding import PartitionSpec as P

TILE = 256
TAPS = 21
PROFILES = 7
WIDTHS = (1.0, 1.0, 1.0, 2.5, 2.5, 2.5, 5.0)
POWERS = (0, 1, 2, 0, 1, 2, 0)
LANES = 128
META = 8

F32 = jnp.float32
BF16 = jnp.bfloat16


def split_np(values):
    values = np.asarray(values, np.float32)
    high = values.astype(BF16)
    low = (values - high.astype(np.float32)).astype(BF16)
    return high, low


def constants(side, basis):
    reach = (TAPS - 1) // 2
    support = np.arange(TAPS).astype(np.float64) - reach
    taps = []
    for number in range(PROFILES):
        sample = support ** POWERS[number] * np.exp(
            -support * support / (2.0 * WIDTHS[number] ** 2)
        )
        taps.append(sample / np.sqrt(np.sum(sample * sample)))
    taps = np.stack(taps)
    places = np.arange(side)
    spacing = places[:, None] - places[None, :]
    inside = np.abs(spacing) <= reach
    across = np.concatenate(
        [np.where(inside, t[np.clip(spacing + reach, 0, TAPS - 1)], 0.0) for t in taps], axis=1
    )
    rows = np.zeros((LANES, PROFILES * side), np.float64)
    for i in range(PROFILES):
        for j in range(PROFILES):
            for t in range(-reach, reach + 1):
                rows[PROFILES * i + j, i * side + t % side] = taps[j, t + reach]
    return split_np(across) + split_np(rows)


def split(values):
    high = values.astype(BF16)
    low = (values - high.astype(F32)).astype(BF16)
    return high, low


def mm(a, b):
    return jnp.dot(a, b, preferred_element_type=F32)


def mm3(a_high, a_low, b_high, b_low):
    return mm(a_high, b_high) + (mm(a_high, b_low) + mm(a_low, b_high))


def spread_along(shape, axis, side):
    places = lax.broadcasted_iota(jnp.int32, shape, axis).astype(F32)
    return (2.0 * places - (side - 1)) / (side - 1)


def tap_rows(coef_ref, coef_buf, tap_buf, rows_high, rows_low, slots):
    coef_buf[...] = jnp.zeros(coef_buf.shape, F32)
    basis = coef_ref.shape[-1]
    for b in range(slots):
        coef_buf[pl.ds(8 * b, 3), pl.ds(0, basis)] = coef_ref[0, b]
    high, low = split(coef_buf[...])
    tap_buf[...] = mm3(high, low, rows_high[...], rows_low[...])


def kernel_pass(block, b, tap_buf, across_high, across_low, left_high, left_low, side):
    reach = (TAPS - 1) // 2
    square = (side, side)
    row = lax.broadcasted_iota(jnp.int32, square, 0)
    col = lax.broadcasted_iota(jnp.int32, square, 1)
    band = jnp.abs(col - row) <= reach
    spread_y = spread_along(square, 0, side)
    for i in range(PROFILES):
        lanes = slice(i * side, (i + 1) * side)
        plain = jnp.broadcast_to(tap_buf[8 * b : 8 * b + 1, lanes], square)
        sideways = jnp.broadcast_to(tap_buf[8 * b + 1 : 8 * b + 2, lanes], square)
        along = jnp.broadcast_to(tap_buf[8 * b + 2 : 8 * b + 3, lanes], square)
        for part, taps in ((0, plain + along * spread_y), (1, sideways)):
            rolled = pltpu.roll(taps, 0, 1, stride=1, stride_axis=0)
            high, low = split(jnp.where(band, rolled, 0.0))
            left_high[part * side : (part + 1) * side, lanes] = high
            left_low[part * side : (part + 1) * side, lanes] = low
    block_high, block_low = split(block)
    across = mm3(block_high, block_low, across_high[...], across_low[...])
    stacked = jnp.concatenate(
        [across[:, i * side : (i + 1) * side] for i in range(PROFILES)], axis=0
    )
    stacked_high, stacked_low = split(stacked)
    both = mm3(left_high[...], left_low[...], stacked_high, stacked_low)
    return both[:side] + both[side:] * spread_along(square, 1, side)


def first_kernel(
    slots, side, tiles, meta_blocks, halves,
    science, coef, rows_high, rows_low, across_high, across_low,
    weight, slot_tile, offsets, counts, tile_place,
    keep, send,
    coef_buf, tap_buf, left_high, left_low, total,
):
    visit = lax.axis_index("visit")
    sky = lax.axis_index("sky")
    core = visit % 2
    half = TILE // 2
    sky_size = tiles
    tap_rows(coef, coef_buf, tap_buf, rows_high, rows_low, slots)
    total[...] = jnp.zeros(total.shape, F32)
    first_lane = (visit * sky_size + sky) * slots
    lane = lax.broadcasted_iota(jnp.int32, (META, LANES), 1)
    field = lax.broadcasted_iota(jnp.int32, (META, LANES), 0)
    meta = [jnp.zeros((META, LANES), F32) for _ in range(meta_blocks)]
    col = lax.broadcasted_iota(jnp.int32, (side, side), 1)
    for b in range(slots):
        owner = tile_place[slot_tile[0, b]]
        usable = b < counts[0, 0]
        used = jnp.where(usable, weight[0, b], 0.0)
        top = offsets[0, b, 0]
        left = offsets[0, b, 1]
        entry = jnp.where(
            field == 0,
            used,
            jnp.where(
                field == 1,
                top.astype(F32),
                jnp.where(field == 2, left.astype(F32), jnp.where(field == 3, owner.astype(F32), 0.0)),
            ),
        )
        for m in range(meta_blocks):
            meta[m] = jnp.where(lane + m * LANES == first_lane + b, entry, meta[m])
        image = kernel_pass(
            science[0, b], b, tap_buf, across_high, across_low, left_high, left_low, side
        )
        image = jnp.where(usable, image * used, 0.0)
        moved = pltpu.roll(image, left, 1)
        total[owner, 0, pl.ds(top, side), :] += jnp.where(col >= left, moved, 0.0)
        total[owner, 1, pl.ds(top, side), :] += jnp.where(col < left, moved, 0.0)
    body = tiles * 2 * half
    for t in range(tiles):
        for h in range(2):
            base = (t * 2 + h) * half
            keep[pl.ds(base, half), :] = total[t, h, pl.ds(core * half, half), :]
            send[pl.ds(base, half), :] = total[t, h, pl.ds((1 - core) * half, half), :]
    for m in range(meta_blocks):
        keep[pl.ds(body + m * META, META), :] = meta[m]
        send[pl.ds(body + m * META, META), :] = meta[m]


def scatter_kernel(tiles, strip, peers, meta_rows, keep, received, *pieces):
    place = lax.axis_index("visit") // 2
    half = strip * peers
    body = tiles * 2 * half
    for j in range(peers):
        first = (place ^ j) * strip
        for g in range(tiles * 2):
            source = pl.ds(g * half + first, strip)
            pieces[j][pl.ds(g * strip, strip), :] = keep[source, :] + received[source, :]
        source = pl.ds(body, meta_rows)
        pieces[j][pl.ds(tiles * 2 * strip, meta_rows), :] = keep[source, :] + received[source, :]


def plane_kernel(tiles, strip, peers, meta_rows, *refs):
    sources, pieces = refs[:peers], refs[peers:]
    sky = lax.axis_index("sky")
    size = 2 * strip
    tail = pl.ds(tiles * size, meta_rows)
    meta = sources[0][tail, :]
    for p in range(1, peers):
        meta = meta + sources[p][tail, :]
    for j in range(tiles):
        rows = pl.ds((sky ^ j) * size, size)
        value = sources[0][rows, :]
        for p in range(1, peers):
            value = value + sources[p][rows, :]
        pieces[j][pl.ds(0, size), :] = value
        pieces[j][pl.ds(size, meta_rows), :] = meta


def template_kernel(tiles, strip, peers, meta_blocks, side, *refs):
    sources, out = refs[:tiles], refs[tiles]
    visit = lax.axis_index("visit")
    sky = lax.axis_index("sky")
    size = 2 * strip
    value = sources[0][...]
    for p in range(1, tiles):
        value = value + sources[p][...]
    first = (visit % 2) * (TILE // 2) + (visit // 2) * strip
    y = (lax.broadcasted_iota(jnp.int32, (strip, LANES), 0) + first).astype(F32)
    x = lax.broadcasted_iota(jnp.int32, (TILE, LANES), 0).astype(F32)
    coverage = jnp.zeros((strip, TILE), F32)
    for m in range(meta_blocks):
        meta = value[size + m * META : size + (m + 1) * META]
        used, top, left, owner = meta[0:1], meta[1:2], meta[2:3], meta[3:4]
        inside = (y >= top) & (y < top + side) & (owner == sky.astype(F32))
        amount = jnp.where(inside, jnp.broadcast_to(used, y.shape), 0.0)
        columns = jnp.where((x >= left) & (x < left + side), 1.0, 0.0).astype(BF16)
        one, rest = split(amount)
        two = (amount - one.astype(F32)).astype(BF16)
        three = (amount - one.astype(F32) - two.astype(F32)).astype(BF16)
        for part in (one, two, three):
            coverage = coverage + lax.dot_general(
                part, columns, (((1,), (1,)), ((), ())), preferred_element_type=F32
            )
    for h in range(2):
        out[pl.ds(h * strip, strip), :] = value[h * strip : (h + 1) * strip] / (
            coverage[:, h * LANES : (h + 1) * LANES] + 1.0
        )


def stack_kernel(tiles, strip, *refs):
    sources, out = refs[:tiles], refs[tiles]
    sky = lax.axis_index("sky")
    size = 2 * strip
    for j in range(tiles):
        out[pl.ds((sky ^ j) * size, size), :] = sources[j][...]


def second_kernel(
    slots, side, tiles, strip, peers,
    science, coef, rows_high, rows_low, across_high, across_low,
    slot_tile, offsets, counts, tile_place,
    *refs,
):
    pieces = refs[: 2 * peers]
    template, difference = refs[2 * peers : 2 * peers + 2]
    coef_buf, tap_buf, left_high, left_low, total = refs[2 * peers + 2 :]
    visit = lax.axis_index("visit")
    sky = lax.axis_index("sky")
    core = visit % 2
    place = visit // 2
    half = TILE // 2
    tap_rows(coef, coef_buf, tap_buf, rows_high, rows_low, slots)
    for c in range(2):
        for j in range(peers):
            first = (core ^ c) * half + (place ^ j) * strip
            for t in range(tiles):
                for h in range(2):
                    total[t, h, pl.ds(first, strip), :] = pieces[c * peers + j][
                        pl.ds((t * 2 + h) * strip, strip), :
                    ]
    for h in range(2):
        template[0, :, h * LANES : (h + 1) * LANES] = total[sky, h]
    col = lax.broadcasted_iota(jnp.int32, (side, side), 1)
    for b in range(slots):
        owner = tile_place[slot_tile[0, b]]
        usable = b < counts[0, 0]
        top = offsets[0, b, 0]
        left = offsets[0, b, 1]
        joined = jnp.where(
            col >= left, total[owner, 0, pl.ds(top, side), :], total[owner, 1, pl.ds(top, side), :]
        )
        cutout = pltpu.roll(joined, (side - left) % side, 1)
        matched = kernel_pass(
            cutout, b, tap_buf, across_high, across_low, left_high, left_low, side
        )
        difference[0, b] = jnp.where(usable, science[0, b] - matched, 0.0)


def body(science, coef_first, coef_second, weight, slot_tile, offsets, counts, tile_place):
    slots, side = science.shape[1], science.shape[2]
    basis = coef_first.shape[-1]
    visits = lax.axis_size("visit")
    tiles = lax.axis_size("sky")
    peers = visits // 2
    strip = TILE // visits
    meta_blocks = -(-visits * tiles * slots // LANES)
    meta_rows = meta_blocks * META
    across_high, across_low, rows_high, rows_low = (
        jnp.asarray(c) for c in constants(side, basis)
    )
    vmem = pl.BlockSpec(memory_space=pltpu.VMEM)
    smem = pl.BlockSpec(memory_space=pltpu.SMEM)

    def shape(*dims):
        return jax.ShapeDtypeStruct(dims, F32)

    def call(function, ins, outs, specs=None, scratch=(), name=None):
        return pl.pallas_call(
            function,
            out_shape=outs,
            in_specs=specs or [vmem] * len(ins),
            out_specs=jax.tree.map(lambda _: vmem, outs),
            scratch_shapes=list(scratch),
            name=name,
        )(*ins)

    scratch = [
        pltpu.VMEM((8 * slots, LANES), F32),
        pltpu.VMEM((8 * slots, PROFILES * side), F32),
        pltpu.VMEM((2 * side, PROFILES * side), BF16),
        pltpu.VMEM((2 * side, PROFILES * side), BF16),
        pltpu.VMEM((tiles, 2, TILE, LANES), F32),
    ]

    def flip(value, axis, size, mask):
        return lax.ppermute(value, axis, [(d, d ^ mask) for d in range(size)])

    keep, send = call(
        lambda *refs: first_kernel(slots, side, tiles, meta_blocks, peers, *refs),
        (science, coef_first, rows_high, rows_low, across_high, across_low,
         weight, slot_tile, offsets, counts, tile_place),
        [shape(tiles * TILE + meta_rows, LANES)] * 2,
        specs=[vmem] * 6 + [smem] * 5,
        scratch=scratch,
        name="first",
    )
    received = flip(send, "visit", visits, 1)
    pieces = call(
        lambda *refs: scatter_kernel(tiles, strip, peers, meta_rows, *refs),
        (keep, received),
        [shape(tiles * 2 * strip + meta_rows, LANES)] * peers,
        name="scatter",
    )
    arrived = [pieces[0]] + [flip(pieces[j], "visit", visits, 2 * j) for j in range(1, peers)]
    pieces = call(
        lambda *refs: plane_kernel(tiles, strip, peers, meta_rows, *refs),
        arrived,
        [shape(2 * strip + meta_rows, LANES)] * tiles,
        name="plane",
    )
    arrived = [pieces[0]] + [flip(pieces[j], "sky", tiles, j) for j in range(1, tiles)]
    strips = call(
        lambda *refs: template_kernel(tiles, strip, peers, meta_blocks, side, *refs),
        arrived,
        shape(2 * strip, LANES),
        name="template",
    )
    strips = [strips] + [flip(strips, "sky", tiles, j) for j in range(1, tiles)]
    piece = call(
        lambda *refs: stack_kernel(tiles, strip, *refs),
        strips,
        shape(tiles * 2 * strip, LANES),
        name="stack",
    )
    mine = [piece] + [flip(piece, "visit", visits, 2 * j) for j in range(1, peers)]
    theirs = [flip(p, "visit", visits, 1) for p in mine]
    template, difference = call(
        lambda *refs: second_kernel(slots, side, tiles, strip, peers, *refs),
        (science, coef_second, rows_high, rows_low, across_high, across_low,
         slot_tile, offsets, counts, tile_place, *mine, *theirs),
        [shape(1, TILE, TILE), shape(1, slots, side, side)],
        specs=[vmem] * 6 + [smem] * 4 + [vmem] * (2 * peers),
        scratch=scratch,
        name="second",
    )
    return template, difference


def solution(mesh):
    in_specs = (
        P("visit", "sky", None, None),
        P("visit", "sky", None, None),
        P("visit", "sky", None, None),
        P("visit", "sky"),
        P("visit", "sky"),
        P("visit", "sky", None),
        P("visit", "sky"),
        P(),
    )
    out_specs = (P("sky", None, None), P("visit", "sky", None, None))
    return jax.shard_map(body, mesh=mesh, in_specs=in_specs, out_specs=out_specs, check_vma=False)
```

```python
import numpy as np
import jax
import jax.numpy as jnp
from jax import lax
from jax.experimental import pallas as pl
from jax.experimental.pallas import tpu as pltpu
from jax.sharding import PartitionSpec as P


TILE = 256
TAPS = 21
PROFILES = 7
WIDTHS = (1.0, 1.0, 1.0, 2.5, 2.5, 2.5, 5.0)
POWERS = (0, 1, 2, 0, 1, 2, 0)
LANES = 128
META = 8
VMEM_BYTES = 24 * 2**20

F32 = jnp.float32
BF16 = jnp.bfloat16


def split_np(values):
    values = np.asarray(values, np.float32)
    high = values.astype(BF16)
    low = (values - high.astype(np.float32)).astype(BF16)
    return high, low


def constants(side):
    reach = (TAPS - 1) // 2
    support = np.arange(TAPS).astype(np.float64) - reach
    taps = []
    for number in range(PROFILES):
        sample = support ** POWERS[number] * np.exp(
            -support * support / (2.0 * WIDTHS[number] ** 2)
        )
        taps.append(sample / np.sqrt(np.sum(sample * sample)))
    taps = np.stack(taps)
    places = np.arange(side)
    spacing = places[:, None] - places[None, :]
    inside = np.abs(spacing) <= reach
    across = np.concatenate(
        [np.where(inside, t[np.clip(spacing + reach, 0, TAPS - 1)], 0.0) for t in taps], axis=1
    )
    rows = np.zeros((LANES, PROFILES * side), np.float64)
    for i in range(PROFILES):
        for j in range(PROFILES):
            for t in range(-reach, reach + 1):
                rows[PROFILES * i + j, i * side + t % side] = taps[j, t + reach]
    return split_np(across) + split_np(rows)


def split(values):
    high = values.astype(BF16)
    low = (values - high.astype(F32)).astype(BF16)
    return high, low


def mm(a, b):
    return jnp.dot(a, b, preferred_element_type=F32)


def mm3(a_high, a_low, b_high, b_low):
    return mm(a_high, b_high) + (mm(a_high, b_low) + mm(a_low, b_high))


def spread_along(shape, axis, side):
    places = lax.broadcasted_iota(jnp.int32, shape, axis).astype(F32)
    return (2.0 * places - (side - 1)) / (side - 1)


def tap_rows(coef_ref, coef_buf, tap_buf, rows_high, rows_low, slots):
    coef_buf[...] = jnp.zeros(coef_buf.shape, F32)
    basis = coef_ref.shape[-1]
    pitch = coef_buf.shape[0] // 3
    for k in range(3):
        coef_buf[pl.ds(pitch * k, slots), pl.ds(0, basis)] = coef_ref[0, k]
    high, low = split(coef_buf[...])
    tap_buf[...] = mm3(high, low, rows_high[...], rows_low[...])


def kernel_pass(block, b, tap_buf, across_high, across_low, left_high, left_low, side):
    reach = (TAPS - 1) // 2
    square = (side, side)
    row = lax.broadcasted_iota(jnp.int32, square, 0)
    col = lax.broadcasted_iota(jnp.int32, square, 1)
    band = jnp.abs(col - row) <= reach
    spread_y = spread_along(square, 0, side)
    pitch = tap_buf.shape[0] // 3
    for i in range(PROFILES):
        lanes = slice(i * side, (i + 1) * side)
        plain = jnp.broadcast_to(tap_buf[b : b + 1, lanes], square)
        sideways = jnp.broadcast_to(tap_buf[pitch + b : pitch + b + 1, lanes], square)
        along = jnp.broadcast_to(tap_buf[2 * pitch + b : 2 * pitch + b + 1, lanes], square)
        for part, taps in ((0, plain + along * spread_y), (1, sideways)):
            rolled = pltpu.roll(taps, 0, 1, stride=1, stride_axis=0)
            high, low = split(jnp.where(band, rolled, 0.0))
            left_high[part * side : (part + 1) * side, lanes] = high
            left_low[part * side : (part + 1) * side, lanes] = low
    block_high, block_low = split(block)
    across = mm3(block_high, block_low, across_high[...], across_low[...])
    stacked = jnp.concatenate(
        [across[:, i * side : (i + 1) * side] for i in range(PROFILES)], axis=0
    )
    stacked_high, stacked_low = split(stacked)
    both = mm3(left_high[...], left_low[...], stacked_high, stacked_low)
    return both[:side] + both[side:] * spread_along(square, 1, side)


def first_kernel(
    slots, side, tiles, meta_blocks,
    science, coef, rows_high, rows_low, across_high, across_low,
    weight, slot_tile, offsets, counts, tile_place,
    keep, send,
    coef_buf, tap_buf, left_high, left_low, total,
):
    visit = lax.axis_index("visit")
    sky = lax.axis_index("sky")
    core = visit % 2
    half = TILE // 2
    sky_size = tiles
    tap_rows(coef, coef_buf, tap_buf, rows_high, rows_low, slots)
    total[...] = jnp.zeros(total.shape, F32)
    first_lane = (visit * sky_size + sky) * slots
    lane = lax.broadcasted_iota(jnp.int32, (META, LANES), 1)
    field = lax.broadcasted_iota(jnp.int32, (META, LANES), 0)
    meta = [jnp.zeros((META, LANES), F32) for _ in range(meta_blocks)]
    col = lax.broadcasted_iota(jnp.int32, (side, side), 1)
    for b in range(slots):
        owner = tile_place[slot_tile[0, b]]
        usable = b < counts[0, 0]
        used = jnp.where(usable, weight[0, b], 0.0)
        top = offsets[0, 0, b]
        left = offsets[0, 1, b]
        entry = jnp.where(
            field == 0,
            used,
            jnp.where(
                field == 1,
                top.astype(F32),
                jnp.where(field == 2, left.astype(F32), jnp.where(field == 3, owner.astype(F32), 0.0)),
            ),
        )
        for m in range(meta_blocks):
            meta[m] = jnp.where(lane + m * LANES == first_lane + b, entry, meta[m])
        image = kernel_pass(
            science[0, b], b, tap_buf, across_high, across_low, left_high, left_low, side
        )
        image = jnp.where(usable, image * used, 0.0)
        moved = pltpu.roll(image, left, 1)
        total[owner, 0, pl.ds(top, side), :] += jnp.where(col >= left, moved, 0.0)
        total[owner, 1, pl.ds(top, side), :] += jnp.where(col < left, moved, 0.0)
    body = tiles * 2 * half
    for t in range(tiles):
        for h in range(2):
            base = (t * 2 + h) * half
            keep[pl.ds(base, half), :] = total[t, h, pl.ds(core * half, half), :]
            send[pl.ds(base, half), :] = total[t, h, pl.ds((1 - core) * half, half), :]
    for m in range(meta_blocks):
        keep[pl.ds(body + m * META, META), :] = meta[m]
        send[pl.ds(body + m * META, META), :] = meta[m]


def scatter_kernel(tiles, strip, peers, meta_rows, keep, received, *pieces):
    pieces = pieces[::-1]
    place = lax.axis_index("visit") // 2
    half = strip * peers
    body = tiles * 2 * half
    for j in range(peers):
        first = (place ^ j) * strip
        for g in range(tiles * 2):
            source = pl.ds(g * half + first, strip)
            pieces[j][pl.ds(g * strip, strip), :] = keep[source, :] + received[source, :]
        source = pl.ds(body, meta_rows)
        pieces[j][pl.ds(tiles * 2 * strip, meta_rows), :] = keep[source, :] + received[source, :]


def plane_kernel(tiles, strip, peers, meta_rows, *refs):
    sources, pieces = refs[:peers], refs[peers:][::-1]
    sky = lax.axis_index("sky")
    size = 2 * strip
    tail = pl.ds(tiles * size, meta_rows)
    meta = sources[0][tail, :]
    for p in range(1, peers):
        meta = meta + sources[p][tail, :]
    for j in range(tiles):
        rows = pl.ds((sky ^ j) * size, size)
        value = sources[0][rows, :]
        for p in range(1, peers):
            value = value + sources[p][rows, :]
        pieces[j][pl.ds(0, size), :] = value
        pieces[j][pl.ds(size, meta_rows), :] = meta


def template_kernel(tiles, strip, meta_blocks, side, *refs):
    sources, out = refs[:tiles], refs[tiles]
    visit = lax.axis_index("visit")
    sky = lax.axis_index("sky")
    size = 2 * strip
    value = sources[0][...]
    for p in range(1, tiles):
        value = value + sources[p][...]
    first = (visit % 2) * (TILE // 2) + (visit // 2) * strip
    y = (lax.broadcasted_iota(jnp.int32, (strip, LANES), 0) + first).astype(F32)
    x = lax.broadcasted_iota(jnp.int32, (TILE, LANES), 0).astype(F32)
    coverage = jnp.zeros((strip, TILE), F32)
    for m in range(meta_blocks):
        meta = value[size + m * META : size + (m + 1) * META]
        used, top, left, owner = meta[0:1], meta[1:2], meta[2:3], meta[3:4]
        inside = (y >= top) & (y < top + side) & (owner == sky.astype(F32))
        amount = jnp.where(inside, jnp.broadcast_to(used, y.shape), 0.0)
        columns = jnp.where((x >= left) & (x < left + side), 1.0, 0.0).astype(BF16)
        one, _ = split(amount)
        two = (amount - one.astype(F32)).astype(BF16)
        three = (amount - one.astype(F32) - two.astype(F32)).astype(BF16)
        for part in (one, two, three):
            coverage = coverage + lax.dot_general(
                part, columns, (((1,), (1,)), ((), ())), preferred_element_type=F32
            )
    for h in range(2):
        out[pl.ds(h * strip, strip), :] = value[h * strip : (h + 1) * strip] / (
            coverage[:, h * LANES : (h + 1) * LANES] + 1.0
        )


def stack_kernel(tiles, strip, *refs):
    sources, out = refs[:tiles], refs[tiles]
    sky = lax.axis_index("sky")
    size = 2 * strip
    for j in range(tiles):
        out[pl.ds((sky ^ j) * size, size), :] = sources[j][...]


def second_kernel(
    slots, side, tiles, strip, peers,
    science, coef, rows_high, rows_low, across_high, across_low,
    slot_tile, offsets, counts, tile_place,
    *refs,
):
    pieces = refs[: 2 * peers]
    template, difference = refs[2 * peers : 2 * peers + 2]
    coef_buf, tap_buf, left_high, left_low, total = refs[2 * peers + 2 :]
    visit = lax.axis_index("visit")
    sky = lax.axis_index("sky")
    core = visit % 2
    place = visit // 2
    half = TILE // 2
    tap_rows(coef, coef_buf, tap_buf, rows_high, rows_low, slots)
    for c in range(2):
        for j in range(peers):
            first = (core ^ c) * half + (place ^ j) * strip
            for t in range(tiles):
                for h in range(2):
                    total[t, h, pl.ds(first, strip), :] = pieces[c * peers + j][
                        pl.ds((t * 2 + h) * strip, strip), :
                    ]
    for h in range(2):
        template[0, :, h * LANES : (h + 1) * LANES] = total[sky, h]
    col = lax.broadcasted_iota(jnp.int32, (side, side), 1)
    for b in range(slots):
        owner = tile_place[slot_tile[0, b]]
        usable = b < counts[0, 0]
        top = offsets[0, 0, b]
        left = offsets[0, 1, b]
        joined = jnp.where(
            col >= left, total[owner, 0, pl.ds(top, side), :], total[owner, 1, pl.ds(top, side), :]
        )
        cutout = pltpu.roll(joined, (side - left) % side, 1)
        matched = kernel_pass(
            cutout, b, tap_buf, across_high, across_low, left_high, left_low, side
        )
        difference[0, b] = jnp.where(usable, science[0, b] - matched, 0.0)


def body(science, coef_first, coef_second, weight, slot_tile, offsets, counts, tile_place):
    slots, side = science.shape[1], science.shape[2]
    visits = lax.axis_size("visit")
    tiles = lax.axis_size("sky")
    peers = visits // 2
    strip = TILE // visits
    meta_blocks = -(-visits * tiles * slots // LANES)
    meta_rows = meta_blocks * META
    across_high, across_low, rows_high, rows_low = (
        jnp.asarray(c) for c in constants(side)
    )
    vmem = pl.BlockSpec(memory_space=pltpu.VMEM)
    smem = pl.BlockSpec(memory_space=pltpu.SMEM)

    coef_first = coef_first.transpose(0, 2, 1, 3)
    coef_second = coef_second.transpose(0, 2, 1, 3)
    offsets = offsets.transpose(0, 2, 1)

    def shape(*dims):
        return pltpu.VMEM(dims, F32)

    def far(value):
        return pltpu.with_memory_space_constraint(value, pltpu.HBM)

    def near(value):
        return pltpu.with_memory_space_constraint(value, pltpu.VMEM)

    def call(function, ins, outs, specs=None, scratch=()):
        return pl.pallas_call(
            function,
            out_shape=outs,
            in_specs=specs or [vmem] * len(ins),
            out_specs=jax.tree.map(lambda _: vmem, outs),
            scratch_shapes=list(scratch),
            compiler_params=pltpu.CompilerParams(vmem_limit_bytes=VMEM_BYTES),
        )(*ins)

    pitch = -(-slots // 8) * 8
    scratch = [
        pltpu.VMEM((3 * pitch, LANES), F32),
        pltpu.VMEM((3 * pitch, PROFILES * side), F32),
        pltpu.VMEM((2 * side, PROFILES * side), BF16),
        pltpu.VMEM((2 * side, PROFILES * side), BF16),
        pltpu.VMEM((tiles, 2, TILE, LANES), F32),
    ]

    def flip(value, axis, size, mask):
        return lax.ppermute(value, axis, [(d, d ^ mask) for d in range(size)])

    def exchange(values, axis, size, step):
        out = [values[0]]
        for j in range(1, len(values)):
            out.append(flip(values[j], axis, size, step * j))
        return out

    keep, send = call(
        lambda *refs: first_kernel(slots, side, tiles, meta_blocks, *refs),
        (*map(far, (science, coef_first, rows_high, rows_low, across_high, across_low)),
         weight, slot_tile, offsets, counts, tile_place),
        [shape(tiles * TILE + meta_rows, LANES)] * 2,
        specs=[vmem] * 6 + [smem] * 5,
        scratch=scratch,
    )
    received = flip(send, "visit", visits, 1)
    pieces = call(
        lambda *refs: scatter_kernel(tiles, strip, peers, meta_rows, *refs),
        (near(keep), near(received)),
        [shape(tiles * 2 * strip + meta_rows, LANES)] * peers,
    )[::-1]
    arrived = exchange(pieces, "visit", visits, 2)
    pieces = call(
        lambda *refs: plane_kernel(tiles, strip, peers, meta_rows, *refs),
        [near(a) for a in arrived],
        [shape(2 * strip + meta_rows, LANES)] * tiles,
    )[::-1]
    arrived = exchange(pieces, "sky", tiles, 1)
    strips = call(
        lambda *refs: template_kernel(tiles, strip, meta_blocks, side, *refs),
        [near(a) for a in arrived],
        shape(2 * strip, LANES),
    )
    strips = exchange([strips] * tiles, "sky", tiles, 1)
    piece = call(
        lambda *refs: stack_kernel(tiles, strip, *refs),
        [near(a) for a in strips],
        shape(tiles * 2 * strip, LANES),
    )
    mine = exchange([piece] * peers, "visit", visits, 2)
    theirs = [flip(p, "visit", visits, 1) for p in mine]
    template, difference = call(
        lambda *refs: second_kernel(slots, side, tiles, strip, peers, *refs),
        (science, coef_second, rows_high, rows_low, across_high, across_low,
         slot_tile, offsets, counts, tile_place, *map(near, mine), *map(near, theirs)),
        [jax.ShapeDtypeStruct(d, F32) for d in ((1, TILE, TILE), (1, slots, side, side))],
        specs=[vmem] * 6 + [smem] * 4 + [vmem] * (2 * peers),
        scratch=scratch,
    )
    return template, difference


def solution(mesh):
    in_specs = (
        P("visit", "sky", None, None),
        P("visit", "sky", None, None),
        P("visit", "sky", None, None),
        P("visit", "sky"),
        P("visit", "sky"),
        P("visit", "sky", None),
        P("visit", "sky"),
        P(),
    )
    out_specs = (P("sky", None, None), P("visit", "sky", None, None))

    return jax.shard_map(body, mesh=mesh, in_specs=in_specs, out_specs=out_specs, check_vma=False)
```

```python
import numpy as np
import jax
import jax.numpy as jnp
from jax import lax
from jax.experimental import pallas as pl
from jax.experimental.pallas import tpu as pltpu
from jax.sharding import PartitionSpec as P


TILE = 256
TAPS = 21
PROFILES = 7
WIDTHS = (1.0, 1.0, 1.0, 2.5, 2.5, 2.5, 5.0)
POWERS = (0, 1, 2, 0, 1, 2, 0)
LANES = 128
META = 8
VMEM_BYTES = 24 * 2**20

F32 = jnp.float32
BF16 = jnp.bfloat16


def split_np(values):
    values = np.asarray(values, np.float32)
    high = values.astype(BF16)
    low = (values - high.astype(np.float32)).astype(BF16)
    return high, low


def constants(side, basis):
    reach = (TAPS - 1) // 2
    support = np.arange(TAPS).astype(np.float64) - reach
    taps = []
    for number in range(PROFILES):
        sample = support ** POWERS[number] * np.exp(
            -support * support / (2.0 * WIDTHS[number] ** 2)
        )
        taps.append(sample / np.sqrt(np.sum(sample * sample)))
    taps = np.stack(taps)
    places = np.arange(side)
    spacing = places[:, None] - places[None, :]
    inside = np.abs(spacing) <= reach
    across = np.concatenate(
        [np.where(inside, t[np.clip(spacing + reach, 0, TAPS - 1)], 0.0) for t in taps], axis=1
    )
    rows = np.zeros((-(-basis // 64) * 64, PROFILES * side), np.float64)
    for i in range(PROFILES):
        for j in range(PROFILES):
            for t in range(-reach, reach + 1):
                rows[PROFILES * i + j, i * side + t % side] = taps[j, t + reach]
    return split_np(across) + split_np(rows)


def row_pitch(slots):
    return -(-slots // 8) * 8


def split(values):
    high = values.astype(BF16)
    low = (values - high.astype(F32)).astype(BF16)
    return high, low


def mm(a, b):
    return jnp.dot(a, b, preferred_element_type=F32)


def spread_along(shape, axis, side):
    places = lax.broadcasted_iota(jnp.int32, shape, axis).astype(F32)
    return (2.0 * places - (side - 1)) / (side - 1)


def tap_rows(coef_ref, coef_buf, tap_buf, rows_high, rows_low, slots):
    coef_buf[...] = jnp.zeros(coef_buf.shape, F32)
    basis = coef_ref.shape[-1]
    depth = rows_high.shape[0]
    pitch = row_pitch(slots)
    rows = coef_buf.shape[0]
    for k in range(3):
        coef_buf[pl.ds(pitch * k, slots), pl.ds(0, basis)] = coef_ref[0, k]
    high, low = split(coef_buf[:, :depth])
    both = mm(jnp.concatenate([high, low], axis=0), rows_high[...])
    tap_buf[...] = both[:rows] + (both[rows:] + mm(high, rows_low[...]))


def build_left(b, slots, side, tap_buf, left):
    reach = (TAPS - 1) // 2
    square = (side, side)
    row = lax.broadcasted_iota(jnp.int32, square, 0)
    col = lax.broadcasted_iota(jnp.int32, square, 1)
    band = jnp.abs(col - row) <= reach
    spread_y = spread_along(square, 0, side)
    pitch = row_pitch(slots)
    for i in range(PROFILES):
        lanes = slice(i * side, (i + 1) * side)
        plain = jnp.broadcast_to(tap_buf[b : b + 1, lanes], square)
        sideways = jnp.broadcast_to(tap_buf[pitch + b : pitch + b + 1, lanes], square)
        along = jnp.broadcast_to(tap_buf[2 * pitch + b : 2 * pitch + b + 1, lanes], square)
        for part, taps in ((0, plain + along * spread_y), (1, sideways)):
            rolled = pltpu.roll(taps, 0, 1, stride=1, stride_axis=0)
            high, low = split(jnp.where(band, rolled, 0.0))
            left[b, part * side : (part + 1) * side, lanes] = high
            left[b, (part + 2) * side : (part + 3) * side, lanes] = low


def put_block(block, b, side, images):
    high, low = split(block)
    images[b * side : (b + 1) * side, :side] = high
    images[b * side : (b + 1) * side, side:] = low


def across_stage(slots, side, images, across_high, across_low, right):
    for first in range(0, PROFILES, 2):
        last = min(first + 2, PROFILES)
        lanes = slice(first * side, last * side)
        high = across_high[:, lanes]
        doubled = jnp.concatenate([high, high], axis=0)
        result = mm(images[...], doubled) + mm(images[:, :side], across_low[:, lanes])
        for i in range(first, last):
            part_high, part_low = split(result[:, (i - first) * side : (i - first + 1) * side])
            for b in range(slots):
                rows = slice(i * side, (i + 1) * side)
                right[b, rows, :side] = part_high[b * side : (b + 1) * side]
                right[b, rows, side:] = part_low[b * side : (b + 1) * side]


def down_stage(b, side, left, right):
    result = mm(left[b], right[b])
    half = 2 * side
    both = result[:half, :side] + (result[:half, side:] + result[half:, :side])
    return both[:side] + both[side:] * spread_along((side, side), 1, side)


def first_kernel(
    slots, side, tiles, meta_blocks,
    science, coef, rows_high, rows_low, across_high, across_low,
    weight, slot_tile, offsets, counts, tile_place,
    keep, send,
    coef_buf, tap_buf, left, images, right, total,
):
    visit = lax.axis_index("visit")
    sky = lax.axis_index("sky")
    core = visit % 2
    half = TILE // 2
    sky_size = tiles
    tap_rows(coef, coef_buf, tap_buf, rows_high, rows_low, slots)
    for b in range(slots):
        put_block(science[0, b], b, side, images)
        build_left(b, slots, side, tap_buf, left)
    across_stage(slots, side, images, across_high, across_low, right)
    total[...] = jnp.zeros(total.shape, F32)
    first_lane = (visit * sky_size + sky) * slots
    lane = lax.broadcasted_iota(jnp.int32, (META, LANES), 1)
    field = lax.broadcasted_iota(jnp.int32, (META, LANES), 0)
    meta = [jnp.zeros((META, LANES), F32) for _ in range(meta_blocks)]
    col = lax.broadcasted_iota(jnp.int32, (side, side), 1)
    for b in range(slots):
        owner = tile_place[slot_tile[0, b]]
        usable = b < counts[0, 0]
        used = jnp.where(usable, weight[0, b], 0.0)
        top = offsets[0, 0, b]
        left_edge = offsets[0, 1, b]
        entry = jnp.where(
            field == 0,
            used,
            jnp.where(
                field == 1,
                top.astype(F32),
                jnp.where(field == 2, left_edge.astype(F32), jnp.where(field == 3, owner.astype(F32), 0.0)),
            ),
        )
        for m in range(meta_blocks):
            meta[m] = jnp.where(lane + m * LANES == first_lane + b, entry, meta[m])
        image = down_stage(b, side, left, right)
        image = jnp.where(usable, image * used, 0.0)
        moved = pltpu.roll(image, left_edge, 1)
        total[owner, 0, pl.ds(top, side), :] += jnp.where(col >= left_edge, moved, 0.0)
        total[owner, 1, pl.ds(top, side), :] += jnp.where(col < left_edge, moved, 0.0)
    body = tiles * 2 * half
    for t in range(tiles):
        for h in range(2):
            base = (t * 2 + h) * half
            keep[pl.ds(base, half), :] = total[t, h, pl.ds(core * half, half), :]
            send[pl.ds(base, half), :] = total[t, h, pl.ds((1 - core) * half, half), :]
    for m in range(meta_blocks):
        keep[pl.ds(body + m * META, META), :] = meta[m]
        send[pl.ds(body + m * META, META), :] = meta[m]


def scatter_kernel(tiles, strip, peers, meta_rows, keep, received, *pieces):
    pieces = pieces[::-1]
    place = lax.axis_index("visit") // 2
    half = strip * peers
    body = tiles * 2 * half
    for j in range(peers):
        first = (place ^ j) * strip
        for g in range(tiles * 2):
            source = pl.ds(g * half + first, strip)
            pieces[j][pl.ds(g * strip, strip), :] = keep[source, :] + received[source, :]
        source = pl.ds(body, meta_rows)
        pieces[j][pl.ds(tiles * 2 * strip, meta_rows), :] = keep[source, :] + received[source, :]


def plane_kernel(tiles, strip, peers, meta_rows, *refs):
    sources, pieces = refs[:peers], refs[peers:][::-1]
    sky = lax.axis_index("sky")
    size = 2 * strip
    tail = pl.ds(tiles * size, meta_rows)
    meta = sources[0][tail, :]
    for p in range(1, peers):
        meta = meta + sources[p][tail, :]
    for j in range(tiles):
        rows = pl.ds((sky ^ j) * size, size)
        value = sources[0][rows, :]
        for p in range(1, peers):
            value = value + sources[p][rows, :]
        pieces[j][pl.ds(0, size), :] = value
        pieces[j][pl.ds(size, meta_rows), :] = meta


def template_kernel(tiles, strip, meta_blocks, side, *refs):
    sources, out = refs[:tiles], refs[tiles]
    visit = lax.axis_index("visit")
    sky = lax.axis_index("sky")
    size = 2 * strip
    value = sources[0][...]
    for p in range(1, tiles):
        value = value + sources[p][...]
    first = (visit % 2) * (TILE // 2) + (visit // 2) * strip
    y = (lax.broadcasted_iota(jnp.int32, (strip, LANES), 0) + first).astype(F32)
    x = lax.broadcasted_iota(jnp.int32, (TILE, LANES), 0).astype(F32)
    coverage = jnp.zeros((strip, TILE), F32)
    for m in range(meta_blocks):
        meta = value[size + m * META : size + (m + 1) * META]
        used, top, left, owner = meta[0:1], meta[1:2], meta[2:3], meta[3:4]
        inside = (y >= top) & (y < top + side) & (owner == sky.astype(F32))
        amount = jnp.where(inside, jnp.broadcast_to(used, y.shape), 0.0)
        columns = jnp.where((x >= left) & (x < left + side), 1.0, 0.0).astype(BF16)
        one, _ = split(amount)
        two = (amount - one.astype(F32)).astype(BF16)
        three = (amount - one.astype(F32) - two.astype(F32)).astype(BF16)
        for part in (one, two, three):
            coverage = coverage + lax.dot_general(
                part, columns, (((1,), (1,)), ((), ())), preferred_element_type=F32
            )
    for h in range(2):
        out[pl.ds(h * strip, strip), :] = value[h * strip : (h + 1) * strip] / (
            coverage[:, h * LANES : (h + 1) * LANES] + 1.0
        )


def stack_kernel(tiles, strip, *refs):
    sources, out = refs[:tiles], refs[tiles]
    sky = lax.axis_index("sky")
    size = 2 * strip
    for j in range(tiles):
        out[pl.ds((sky ^ j) * size, size), :] = sources[j][...]


def second_kernel(
    slots, side, tiles, strip, peers,
    science, left, across_high, across_low,
    slot_tile, offsets, counts, tile_place,
    *refs,
):
    pieces = refs[: 2 * peers]
    template, difference = refs[2 * peers : 2 * peers + 2]
    images, right, total = refs[2 * peers + 2 :]
    visit = lax.axis_index("visit")
    sky = lax.axis_index("sky")
    core = visit % 2
    place = visit // 2
    half = TILE // 2
    for c in range(2):
        for j in range(peers):
            first = (core ^ c) * half + (place ^ j) * strip
            for t in range(tiles):
                for h in range(2):
                    total[t, h, pl.ds(first, strip), :] = pieces[c * peers + j][
                        pl.ds((t * 2 + h) * strip, strip), :
                    ]
    for h in range(2):
        template[0, :, h * LANES : (h + 1) * LANES] = total[sky, h]
    col = lax.broadcasted_iota(jnp.int32, (side, side), 1)
    for b in range(slots):
        owner = tile_place[slot_tile[0, b]]
        top = offsets[0, 0, b]
        left_edge = offsets[0, 1, b]
        joined = jnp.where(
            col >= left_edge, total[owner, 0, pl.ds(top, side), :], total[owner, 1, pl.ds(top, side), :]
        )
        put_block(pltpu.roll(joined, (side - left_edge) % side, 1), b, side, images)
    across_stage(slots, side, images, across_high, across_low, right)
    for b in range(slots):
        matched = down_stage(b, side, left, right)
        difference[0, b] = jnp.where(b < counts[0, 0], science[0, b] - matched, 0.0)


def prepare_kernel(slots, side, coef, rows_high, rows_low, left, coef_buf, tap_buf):
    tap_rows(coef, coef_buf, tap_buf, rows_high, rows_low, slots)
    for b in range(slots):
        build_left(b, slots, side, tap_buf, left)


def body(science, coef_first, coef_second, weight, slot_tile, offsets, counts, tile_place):
    slots, side = science.shape[1], science.shape[2]
    basis = coef_first.shape[-1]
    visits = lax.axis_size("visit")
    tiles = lax.axis_size("sky")
    peers = visits // 2
    strip = TILE // visits
    meta_blocks = -(-visits * tiles * slots // LANES)
    meta_rows = meta_blocks * META
    across_high, across_low, rows_high, rows_low = (
        jnp.asarray(c) for c in constants(side, basis)
    )
    vmem = pl.BlockSpec(memory_space=pltpu.VMEM)
    smem = pl.BlockSpec(memory_space=pltpu.SMEM)

    coef_first = coef_first.transpose(0, 2, 1, 3)
    coef_second = coef_second.transpose(0, 2, 1, 3)
    offsets = offsets.transpose(0, 2, 1)

    def shape(*dims):
        return pltpu.VMEM(dims, F32)

    def far(value):
        return pltpu.with_memory_space_constraint(value, pltpu.HBM)

    def near(value):
        return pltpu.with_memory_space_constraint(value, pltpu.VMEM)

    def call(function, ins, outs, specs=None, scratch=()):
        return pl.pallas_call(
            function,
            out_shape=outs,
            in_specs=specs or [vmem] * len(ins),
            out_specs=jax.tree.map(lambda _: vmem, outs),
            scratch_shapes=list(scratch),
            compiler_params=pltpu.CompilerParams(vmem_limit_bytes=VMEM_BYTES),
        )(*ins)

    tap_scratch = [
        pltpu.VMEM((-(-3 * row_pitch(slots) // 16) * 16, LANES), F32),
        pltpu.VMEM((-(-3 * row_pitch(slots) // 16) * 16, PROFILES * side), F32),
    ]
    left_shape = (slots, 4 * side, PROFILES * side)
    pass_scratch = [
        pltpu.VMEM((slots * side, 2 * side), BF16),
        pltpu.VMEM((slots, PROFILES * side, 2 * side), BF16),
        pltpu.VMEM((tiles, 2, TILE, LANES), F32),
    ]

    def flip(value, axis, size, mask):
        return lax.ppermute(value, axis, [(d, d ^ mask) for d in range(size)])

    def exchange(values, axis, size, step):
        out = [values[0]]
        for j in range(1, len(values)):
            out.append(flip(values[j], axis, size, step * j))
        return out

    keep, send = call(
        lambda *refs: first_kernel(slots, side, tiles, meta_blocks, *refs),
        (*map(far, (science, coef_first, rows_high, rows_low, across_high, across_low)),
         *map(far, (weight, slot_tile, offsets)), counts, far(tile_place)),
        [shape(tiles * TILE + meta_rows, LANES)] * 2,
        specs=[vmem] * 6 + [smem] * 5,
        scratch=tap_scratch + [pltpu.VMEM(left_shape, BF16)] + pass_scratch,
    )
    left = call(
        lambda *refs: prepare_kernel(slots, side, *refs),
        (coef_second, rows_high, rows_low),
        pltpu.VMEM(left_shape, BF16),
        scratch=tap_scratch,
    )
    received = flip(send, "visit", visits, 1)
    pieces = call(
        lambda *refs: scatter_kernel(tiles, strip, peers, meta_rows, *refs),
        (near(keep), near(received)),
        [shape(tiles * 2 * strip + meta_rows, LANES)] * peers,
    )[::-1]
    arrived = exchange(pieces, "visit", visits, 2)
    pieces = call(
        lambda *refs: plane_kernel(tiles, strip, peers, meta_rows, *refs),
        [near(a) for a in arrived],
        [shape(2 * strip + meta_rows, LANES)] * tiles,
    )[::-1]
    arrived = exchange(pieces, "sky", tiles, 1)
    strips = call(
        lambda *refs: template_kernel(tiles, strip, meta_blocks, side, *refs),
        [near(a) for a in arrived],
        shape(2 * strip, LANES),
    )
    strips = exchange([strips] * tiles, "sky", tiles, 1)
    piece = call(
        lambda *refs: stack_kernel(tiles, strip, *refs),
        [near(a) for a in strips],
        shape(tiles * 2 * strip, LANES),
    )
    mine = exchange([piece] * peers, "visit", visits, 2)
    theirs = [flip(p, "visit", visits, 1) for p in mine]
    template, difference = call(
        lambda *refs: second_kernel(slots, side, tiles, strip, peers, *refs),
        (science, near(left), across_high, across_low,
         slot_tile, offsets, counts, tile_place, *map(near, mine), *map(near, theirs)),
        [jax.ShapeDtypeStruct(d, F32) for d in ((1, TILE, TILE), (1, slots, side, side))],
        specs=[vmem] * 4 + [smem] * 4 + [vmem] * (2 * peers),
        scratch=pass_scratch,
    )
    return template, difference


def solution(mesh):
    in_specs = (
        P("visit", "sky", None, None),
        P("visit", "sky", None, None),
        P("visit", "sky", None, None),
        P("visit", "sky"),
        P("visit", "sky"),
        P("visit", "sky", None),
        P("visit", "sky"),
        P(),
    )
    out_specs = (P("sky", None, None), P("visit", "sky", None, None))

    return jax.shard_map(body, mesh=mesh, in_specs=in_specs, out_specs=out_specs, check_vma=False)
```

```python
import numpy as np
import jax
import jax.numpy as jnp
from jax import lax
from jax.experimental import pallas as pl
from jax.experimental.pallas import tpu as pltpu
from jax.sharding import PartitionSpec as P


TILE = 256
TAPS = 21
PROFILES = 7
WIDTHS = (1.0, 1.0, 1.0, 2.5, 2.5, 2.5, 5.0)
POWERS = (0, 1, 2, 0, 1, 2, 0)
LANES = 128
META = 8
VMEM_BYTES = 24 * 2**20

F32 = jnp.float32
BF16 = jnp.bfloat16


def split_np(values):
    values = np.asarray(values, np.float32)
    high = values.astype(BF16)
    low = (values - high.astype(np.float32)).astype(BF16)
    return high, low


def constants(side, basis):
    reach = (TAPS - 1) // 2
    support = np.arange(TAPS).astype(np.float64) - reach
    taps = []
    for number in range(PROFILES):
        sample = support ** POWERS[number] * np.exp(
            -support * support / (2.0 * WIDTHS[number] ** 2)
        )
        taps.append(sample / np.sqrt(np.sum(sample * sample)))
    taps = np.stack(taps)
    places = np.arange(side)
    spacing = places[:, None] - places[None, :]
    inside = np.abs(spacing) <= reach
    across = np.concatenate(
        [np.where(inside, t[np.clip(spacing + reach, 0, TAPS - 1)], 0.0) for t in taps], axis=1
    )
    rows = np.zeros((-(-basis // 64) * 64, PROFILES * side), np.float64)
    for i in range(PROFILES):
        for j in range(PROFILES):
            for t in range(-reach, reach + 1):
                rows[PROFILES * i + j, i * side + t % side] = taps[j, t + reach]
    return split_np(across) + split_np(rows)


def row_pitch(slots):
    return -(-slots // 8) * 8


def split(values):
    high = values.astype(BF16)
    low = (values - high.astype(F32)).astype(BF16)
    return high, low


def mm(a, b):
    return jnp.dot(a, b, preferred_element_type=F32)


def spread_along(shape, axis, side):
    places = lax.broadcasted_iota(jnp.int32, shape, axis).astype(F32)
    return (2.0 * places - (side - 1)) / (side - 1)


def tap_rows(coef_ref, coef_buf, tap_buf, rows_high, rows_low, slots):
    coef_buf[...] = jnp.zeros(coef_buf.shape, F32)
    basis = coef_ref.shape[-1]
    depth = rows_high.shape[0]
    pitch = row_pitch(slots)
    rows = coef_buf.shape[0]
    for k in range(3):
        coef_buf[pl.ds(pitch * k, slots), pl.ds(0, basis)] = coef_ref[0, k]
    high, low = split(coef_buf[:, :depth])
    both = mm(jnp.concatenate([high, low], axis=0), rows_high[...])
    tap_buf[...] = both[:rows] + (both[rows:] + mm(high, rows_low[...]))


def build_left(b, slots, side, tap_buf, left):
    reach = (TAPS - 1) // 2
    square = (side, side)
    row = lax.broadcasted_iota(jnp.int32, square, 0)
    col = lax.broadcasted_iota(jnp.int32, square, 1)
    band = jnp.abs(col - row) <= reach
    spread_y = spread_along(square, 0, side)
    pitch = row_pitch(slots)
    for i in range(PROFILES):
        lanes = slice(i * side, (i + 1) * side)
        plain = jnp.broadcast_to(tap_buf[b : b + 1, lanes], square)
        sideways = jnp.broadcast_to(tap_buf[pitch + b : pitch + b + 1, lanes], square)
        along = jnp.broadcast_to(tap_buf[2 * pitch + b : 2 * pitch + b + 1, lanes], square)
        for part, taps in ((0, plain + along * spread_y), (1, sideways)):
            rolled = pltpu.roll(taps, 0, 1, stride=1, stride_axis=0)
            high, low = split(jnp.where(band, rolled, 0.0))
            left[b, part * side : (part + 1) * side, lanes] = high
            left[b, (part + 2) * side : (part + 3) * side, lanes] = low


def put_block(block, b, side, images):
    high, low = split(block)
    images[b * side : (b + 1) * side, :side] = high
    images[b * side : (b + 1) * side, side:] = low


def across_stage(slots, side, images, across_high, across_low, right):
    for first in range(0, PROFILES, 2):
        last = min(first + 2, PROFILES)
        lanes = slice(first * side, last * side)
        high = across_high[:, lanes]
        doubled = jnp.concatenate([high, high], axis=0)
        result = mm(images[...], doubled) + mm(images[:, :side], across_low[:, lanes])
        for i in range(first, last):
            part_high, part_low = split(result[:, (i - first) * side : (i - first + 1) * side])
            for b in range(slots):
                rows = slice(i * side, (i + 1) * side)
                right[b, rows, :side] = part_high[b * side : (b + 1) * side]
                right[b, rows, side:] = part_low[b * side : (b + 1) * side]


def down_stage(b, side, left, right):
    result = mm(left[b], right[b])
    half = 2 * side
    both = result[:half, :side] + (result[:half, side:] + result[half:, :side])
    return both[:side] + both[side:] * spread_along((side, side), 1, side)


FIRST_FAR = 10
SECOND_FAR = 4


def fetch(sources, targets, semaphores):
    copies = [
        pltpu.make_async_copy(source, target, semaphores.at[n])
        for n, (source, target) in enumerate(zip(sources, targets, strict=True))
    ]
    for copy in copies:
        copy.start()

    def wait(*numbers):
        for n in numbers:
            copies[n].wait()

    return wait, targets


def first_kernel(
    slots, side, tiles, meta_blocks, visits,
    *refs,
):
    far, counts, keep, send = refs[:FIRST_FAR], *refs[FIRST_FAR : FIRST_FAR + 3]
    coef_buf, tap_buf, left, images, right, moved = refs[FIRST_FAR + 3 : FIRST_FAR + 9]
    wait, near = fetch(far, refs[FIRST_FAR + 9 : -1], refs[-1])
    coef, rows_high, rows_low, science, across_high, across_low = near[:6]
    weight, slot_tile, offsets, tile_place = near[6:]
    visit = lax.axis_index("visit")
    sky = lax.axis_index("sky")
    core = visit % 2
    peers = visits // 2
    share = side // visits
    wait(*range(FIRST_FAR))
    tap_rows(coef, coef_buf, tap_buf, rows_high, rows_low, slots)
    for b in range(slots):
        put_block(science[0, b], b, side, images)
        build_left(b, slots, side, tap_buf, left)
    across_stage(slots, side, images, across_high, across_low, right)
    first_lane = (visit * tiles + sky) * slots
    lane = lax.broadcasted_iota(jnp.int32, (META, LANES), 1)
    field = lax.broadcasted_iota(jnp.int32, (META, LANES), 0)
    meta = [jnp.zeros((META, LANES), F32) for _ in range(meta_blocks)]
    for b in range(slots):
        owner = tile_place[slot_tile[0, b]]
        usable = b < counts[0, 0]
        used = jnp.where(usable, weight[0, b], 0.0)
        top = offsets[0, 0, b]
        left_edge = offsets[0, 1, b]
        entry = jnp.where(
            field == 0,
            used,
            jnp.where(
                field == 1,
                top.astype(F32),
                jnp.where(field == 2, left_edge.astype(F32), jnp.where(field == 3, owner.astype(F32), 0.0)),
            ),
        )
        for m in range(meta_blocks):
            meta[m] = jnp.where(lane + m * LANES == first_lane + b, entry, meta[m])
        image = down_stage(b, side, left, right)
        image = jnp.where(usable, image * used, 0.0)
        moved[b] = pltpu.roll(image, left_edge, 1)
        for h, out in ((0, keep), (1, send)):

            def pick(q, b=b, h=h, out=out, top=top):
                residue = 2 * q + (core ^ h)
                start = first_row(top, residue, visits) * visits + residue - top
                out[pl.ds((q * slots + b) * share, share), :] = moved[
                    b, pl.ds(start, share, stride=visits), :
                ]

            repeat(peers, peers, pick)
    body = peers * slots * share
    for m in range(meta_blocks):
        keep[pl.ds(body + m * META, META), :] = meta[m]
        send[pl.ds(body + m * META, META), :] = meta[m]


def quotient(value, divisor):
    if divisor & (divisor - 1) == 0:
        return value >> (divisor.bit_length() - 1)
    return lax.div(value, divisor)


def repeat(count, width, step):
    if width <= 4:
        for n in range(count):
            step(n)
    else:
        lax.fori_loop(0, count, lambda n, carry: (step(n), carry)[1], 0)


def first_row(top, residue, visits):
    return quotient(top - residue + (visits - 1), visits)


def scatter_kernel(rows, peers, meta_rows, keep, received, *pieces):
    place = lax.axis_index("visit") // 2
    tail = pl.ds(peers * rows, meta_rows)
    meta = keep[tail, :] + received[tail, :]
    for j in range(peers):
        source = pl.ds((place ^ j) * rows, rows)
        pieces[j][pl.ds(0, rows), :] = keep[source, :]
        pieces[j][pl.ds(rows, rows), :] = received[source, :]
        pieces[j][pl.ds(2 * rows, meta_rows), :] = meta


def plane_kernel(slots, side, tiles, visits, meta_rows, *refs):
    peers = visits // 2
    share = side // visits
    size = 2 * (TILE // visits)
    sources, pieces = refs[:peers], refs[peers : peers + tiles]
    table, scalars, semaphore = refs[peers + tiles : peers + tiles + 3]
    sums = refs[peers + tiles + 3 :]
    visit = lax.axis_index("visit")
    sky = lax.axis_index("sky")
    core = visit % 2
    place = visit // 2
    tail = pl.ds(2 * slots * share, meta_rows)
    meta = sources[0][tail, :]
    for p in range(1, peers):
        meta = meta + sources[p][tail, :]
    table[...] = meta
    copy = pltpu.make_async_copy(table, scalars, semaphore)
    copy.start()
    for total in sums:
        total[...] = jnp.zeros(total.shape, F32)
    col = lax.broadcasted_iota(jnp.int32, (share, LANES), 1)
    copy.wait()

    def place_rows(h, b):
        for p in range(peers):
            total = sums[p % len(sums)]
            sender = 2 * (place ^ p) + (core ^ h)
            slot = (sender * tiles + sky) * slots + b
            base, lane = 0, slot
            if meta_rows > META:
                base = quotient(slot, LANES)
                lane = slot - base * LANES
                base = base * META
            top = scalars[base + 1, lane].astype(jnp.int32)
            left_edge = scalars[base + 2, lane].astype(jnp.int32)
            owner = scalars[base + 3, lane].astype(jnp.int32)
            rows = sources[p][pl.ds((h * slots + b) * share, share), :]
            where = pl.ds(first_row(top, visit, visits), share)
            total[owner, 0, where, :] += jnp.where(col >= left_edge, rows, 0.0)
            total[owner, 1, where, :] += jnp.where(col < left_edge, rows, 0.0)

    for h in range(2):
        repeat(slots, peers, lambda b, h=h: place_rows(h, b))
    for j in range(tiles):
        tile = sky ^ j
        for h in range(2):
            value = sums[0][tile, h]
            for total in sums[1:]:
                value = value + total[tile, h]
            pieces[j][pl.ds(h * (size // 2), size // 2), :] = value
        pieces[j][pl.ds(size, meta_rows), :] = meta


def template_kernel(tiles, strip, visits, meta_blocks, side, *refs):
    sources, out = refs[:tiles], refs[tiles]
    visit = lax.axis_index("visit")
    sky = lax.axis_index("sky")
    size = 2 * strip
    value = sources[0][...]
    for p in range(1, tiles):
        value = value + sources[p][...]
    y = (lax.broadcasted_iota(jnp.int32, (strip, LANES), 0) * visits + visit).astype(F32)
    x = lax.broadcasted_iota(jnp.int32, (TILE, LANES), 0).astype(F32)
    coverage = jnp.zeros((strip, TILE), F32)
    for m in range(meta_blocks):
        meta = value[size + m * META : size + (m + 1) * META]
        used, top, left, owner = meta[0:1], meta[1:2], meta[2:3], meta[3:4]
        inside = (y >= top) & (y < top + side) & (owner == sky.astype(F32))
        amount = jnp.where(inside, jnp.broadcast_to(used, y.shape), 0.0)
        columns = jnp.where((x >= left) & (x < left + side), 1.0, 0.0).astype(BF16)
        one, _ = split(amount)
        two = (amount - one.astype(F32)).astype(BF16)
        three = (amount - one.astype(F32) - two.astype(F32)).astype(BF16)
        for part in (one, two, three):
            coverage = coverage + lax.dot_general(
                part, columns, (((1,), (1,)), ((), ())), preferred_element_type=F32
            )
    for h in range(2):
        out[pl.ds(h * strip, strip), :] = value[h * strip : (h + 1) * strip] / (
            coverage[:, h * LANES : (h + 1) * LANES] + 1.0
        )


def stack_kernel(tiles, strip, *refs):
    sources, out = refs[:tiles], refs[tiles]
    sky = lax.axis_index("sky")
    size = 2 * strip
    for j in range(tiles):
        out[pl.ds((sky ^ j) * size, size), :] = sources[j][...]


def second_kernel(
    slots, side, tiles, strip, peers,
    left, across_high, across_low, counts,
    *refs,
):
    far, refs = refs[:SECOND_FAR], refs[SECOND_FAR:]
    pieces, refs = refs[: 2 * peers], refs[2 * peers :]
    template, difference, images, right, total, staged, results = refs[:7]
    wait, near = fetch(far, refs[7 : 7 + SECOND_FAR], refs[-2])
    slot_tile, offsets, tile_place, science = near
    outward = refs[-1]
    visit = lax.axis_index("visit")
    sky = lax.axis_index("sky")
    core = visit % 2
    place = visit // 2
    for c in range(2):
        for j in range(peers):
            residue = 2 * (place ^ j) + (core ^ c)
            piece = pieces[c * peers + j]

            def spread_rows(t, residue=residue, piece=piece):
                for h in range(2):
                    total[t, h, pl.ds(residue, strip, stride=2 * peers), :] = piece[
                        pl.ds((t * 2 + h) * strip, strip), :
                    ]

            repeat(tiles, peers, spread_rows)
    for h in range(2):
        staged[:, h * LANES : (h + 1) * LANES] = total[sky, h]
    copies = [pltpu.make_async_copy(staged, template.at[0], outward.at[slots])]
    copies[0].start()
    wait(*range(SECOND_FAR))
    col = lax.broadcasted_iota(jnp.int32, (side, side), 1)
    for b in range(slots):
        owner = tile_place[slot_tile[0, b]]
        top = offsets[0, 0, b]
        left_edge = offsets[0, 1, b]
        joined = jnp.where(
            col >= left_edge, total[owner, 0, pl.ds(top, side), :], total[owner, 1, pl.ds(top, side), :]
        )
        put_block(pltpu.roll(joined, (side - left_edge) % side, 1), b, side, images)
    across_stage(slots, side, images, across_high, across_low, right)
    for b in range(slots):
        matched = down_stage(b, side, left, right)
        results[b] = jnp.where(b < counts[0, 0], science[0, b] - matched, 0.0)
        copies.append(pltpu.make_async_copy(results.at[b], difference.at[0, b], outward.at[b]))
        copies[-1].start()
    for copy in copies:
        copy.wait()


def prepare_kernel(slots, side, coef, rows_high, rows_low, left, coef_buf, tap_buf):
    tap_rows(coef, coef_buf, tap_buf, rows_high, rows_low, slots)
    for b in range(slots):
        build_left(b, slots, side, tap_buf, left)


def body(science, coef_first, coef_second, weight, slot_tile, offsets, counts, tile_place):
    slots, side = science.shape[1], science.shape[2]
    basis = coef_first.shape[-1]
    visits = lax.axis_size("visit")
    tiles = lax.axis_size("sky")
    peers = visits // 2
    strip = TILE // visits
    rows = slots * (side // visits)
    meta_blocks = -(-visits * tiles * slots // LANES)
    meta_rows = meta_blocks * META
    across_high, across_low, rows_high, rows_low = (
        jnp.asarray(c) for c in constants(side, basis)
    )
    vmem = pl.BlockSpec(memory_space=pltpu.VMEM)
    smem = pl.BlockSpec(memory_space=pltpu.SMEM)
    anywhere = pl.BlockSpec(memory_space=pl.ANY)

    coef_first = coef_first.transpose(0, 2, 1, 3)
    coef_second = coef_second.transpose(0, 2, 1, 3)
    offsets = offsets.transpose(0, 2, 1)

    def shape(*dims):
        return pltpu.VMEM(dims, F32)

    def far(value):
        return pltpu.with_memory_space_constraint(value, pltpu.HBM)

    def near(value):
        return pltpu.with_memory_space_constraint(value, pltpu.VMEM)

    def call(function, ins, outs, specs=None, scratch=(), out_space=vmem):
        return pl.pallas_call(
            function,
            out_shape=outs,
            in_specs=specs or [vmem] * len(ins),
            out_specs=jax.tree.map(lambda _: out_space, outs),
            scratch_shapes=list(scratch),
            compiler_params=pltpu.CompilerParams(vmem_limit_bytes=VMEM_BYTES),
        )(*ins)

    tap_scratch = [
        pltpu.VMEM((-(-3 * row_pitch(slots) // 16) * 16, LANES), F32),
        pltpu.VMEM((-(-3 * row_pitch(slots) // 16) * 16, PROFILES * side), F32),
    ]
    left_shape = (slots, 4 * side, PROFILES * side)
    pass_scratch = [
        pltpu.VMEM((slots * side, 2 * side), BF16),
        pltpu.VMEM((slots, PROFILES * side, 2 * side), BF16),
        pltpu.VMEM((tiles, 2, TILE, LANES), F32),
    ]

    def flip(value, axis, size, mask):
        return lax.ppermute(value, axis, [(d, d ^ mask) for d in range(size)])

    def exchange(values, axis, size, step):
        out = [values[0]]
        for j in range(1, len(values)):
            out.append(flip(values[j], axis, size, step * j))
        return out

    first_far = (
        coef_first, rows_high, rows_low, science, across_high, across_low,
        weight, slot_tile, offsets, tile_place,
    )
    keep, send = call(
        lambda *refs: first_kernel(slots, side, tiles, meta_blocks, visits, *refs),
        (*map(far, first_far), counts),
        [shape(peers * rows + meta_rows, LANES)] * 2,
        specs=[anywhere] * FIRST_FAR + [smem],
        scratch=tap_scratch
        + [pltpu.VMEM(left_shape, BF16)]
        + pass_scratch[:2]
        + [pltpu.VMEM((slots, side, LANES), F32)]
        + [pltpu.VMEM(a.shape, a.dtype) for a in first_far[:6]]
        + [pltpu.SMEM(a.shape, a.dtype) for a in first_far[6:]]
        + [pltpu.SemaphoreType.DMA((FIRST_FAR,))],
    )
    left = call(
        lambda *refs: prepare_kernel(slots, side, *refs),
        (far(coef_second), far(rows_high), far(rows_low)),
        pltpu.VMEM(left_shape, BF16),
        scratch=tap_scratch,
    )
    received = flip(send, "visit", visits, 1)
    pieces = call(
        lambda *refs: scatter_kernel(rows, peers, meta_rows, *refs),
        (near(keep), near(received)),
        [shape(2 * rows + meta_rows, LANES)] * peers,
    )
    arrived = exchange(pieces, "visit", visits, 2)
    pieces = call(
        lambda *refs: plane_kernel(slots, side, tiles, visits, meta_rows, *refs),
        [near(a) for a in arrived],
        [shape(2 * strip + meta_rows, LANES)] * tiles,
        scratch=[
            pltpu.VMEM((meta_rows, LANES), F32),
            pltpu.SMEM((meta_rows, LANES), F32),
            pltpu.SemaphoreType.DMA,
        ]
        + [pltpu.VMEM((tiles, 2, strip, LANES), F32)] * min(peers, 4),
    )
    arrived = exchange(pieces, "sky", tiles, 1)
    strips = call(
        lambda *refs: template_kernel(tiles, strip, visits, meta_blocks, side, *refs),
        [near(a) for a in arrived],
        shape(2 * strip, LANES),
    )
    strips = exchange([strips] * tiles, "sky", tiles, 1)
    piece = call(
        lambda *refs: stack_kernel(tiles, strip, *refs),
        [near(a) for a in strips],
        shape(tiles * 2 * strip, LANES),
    )
    mine = exchange([piece] * peers, "visit", visits, 2)
    theirs = [flip(p, "visit", visits, 1) for p in mine]
    second_far = (slot_tile, offsets, tile_place, science)
    template, difference = call(
        lambda *refs: second_kernel(slots, side, tiles, strip, peers, *refs),
        (near(left), near(across_high), near(across_low), counts,
         *map(far, second_far), *map(near, mine), *map(near, theirs)),
        [jax.ShapeDtypeStruct(d, F32) for d in ((1, TILE, TILE), (1, slots, side, side))],
        specs=[vmem] * 3 + [smem] + [anywhere] * SECOND_FAR + [vmem] * (2 * peers),
        scratch=pass_scratch
        + [pltpu.VMEM((TILE, TILE), F32), pltpu.VMEM((slots, side, side), F32)]
        + [pltpu.SMEM(a.shape, a.dtype) for a in second_far[:3]]
        + [pltpu.VMEM(a.shape, a.dtype) for a in second_far[3:]]
        + [pltpu.SemaphoreType.DMA((SECOND_FAR,)), pltpu.SemaphoreType.DMA((slots + 1,))],
        out_space=anywhere,
    )
    return template, difference


def solution(mesh):
    in_specs = (
        P("visit", "sky", None, None),
        P("visit", "sky", None, None),
        P("visit", "sky", None, None),
        P("visit", "sky"),
        P("visit", "sky"),
        P("visit", "sky", None),
        P("visit", "sky"),
        P(),
    )
    out_specs = (P("sky", None, None), P("visit", "sky", None, None))

    return jax.shard_map(body, mesh=mesh, in_specs=in_specs, out_specs=out_specs, check_vma=False)
```

```python
import numpy as np
import jax
import jax.numpy as jnp
from jax import lax
from jax.experimental import pallas as pl
from jax.experimental.pallas import tpu as pltpu
from jax.sharding import PartitionSpec as P


TILE = 256
TAPS = 21
PROFILES = 7
WIDTHS = (1.0, 1.0, 1.0, 2.5, 2.5, 2.5, 5.0)
POWERS = (0, 1, 2, 0, 1, 2, 0)
LANES = 128
META = 8
VMEM_BYTES = 24 * 2**20

F32 = jnp.float32
BF16 = jnp.bfloat16


def split_np(values):
    values = np.asarray(values, np.float32)
    high = values.astype(BF16)
    low = (values - high.astype(np.float32)).astype(BF16)
    return high, low


def constants(side, basis):
    reach = (TAPS - 1) // 2
    support = np.arange(TAPS).astype(np.float64) - reach
    taps = []
    for number in range(PROFILES):
        sample = support ** POWERS[number] * np.exp(
            -support * support / (2.0 * WIDTHS[number] ** 2)
        )
        taps.append(sample / np.sqrt(np.sum(sample * sample)))
    taps = np.stack(taps)
    places = np.arange(side)
    spacing = places[:, None] - places[None, :]
    inside = np.abs(spacing) <= reach
    across = np.concatenate(
        [np.where(inside, t[np.clip(spacing + reach, 0, TAPS - 1)], 0.0) for t in taps], axis=1
    )
    rows = np.zeros((-(-basis // 64) * 64, PROFILES * side), np.float64)
    for i in range(PROFILES):
        for j in range(PROFILES):
            for t in range(-reach, reach + 1):
                rows[PROFILES * i + j, i * side + t % side] = taps[j, t + reach]
    return split_np(across) + split_np(rows)


def row_pitch(slots):
    return -(-slots // 8) * 8


def split(values):
    high = values.astype(BF16)
    low = (values - high.astype(F32)).astype(BF16)
    return high, low


def mm(a, b):
    return jnp.dot(a, b, preferred_element_type=F32)


def spread_along(shape, axis, side):
    places = lax.broadcasted_iota(jnp.int32, shape, axis).astype(F32)
    return (2.0 * places - (side - 1)) / (side - 1)


def tap_rows(coef_ref, coef_buf, tap_buf, rows_high, rows_low, slots):
    coef_buf[...] = jnp.zeros(coef_buf.shape, F32)
    basis = coef_ref.shape[-1]
    depth = rows_high.shape[0]
    pitch = row_pitch(slots)
    rows = coef_buf.shape[0]
    for k in range(3):
        coef_buf[pl.ds(pitch * k, slots), pl.ds(0, basis)] = coef_ref[0, k]
    high, low = split(coef_buf[:, :depth])
    both = mm(jnp.concatenate([high, low], axis=0), rows_high[...])
    tap_buf[...] = both[:rows] + (both[rows:] + mm(high, rows_low[...]))


def build_left(b, slots, side, tap_buf, left):
    reach = (TAPS - 1) // 2
    square = (side, side)
    row = lax.broadcasted_iota(jnp.int32, square, 0)
    col = lax.broadcasted_iota(jnp.int32, square, 1)
    band = jnp.abs(col - row) <= reach
    spread_y = spread_along(square, 0, side)
    pitch = row_pitch(slots)
    for i in range(PROFILES):
        lanes = slice(i * side, (i + 1) * side)
        plain = jnp.broadcast_to(tap_buf[b : b + 1, lanes], square)
        sideways = jnp.broadcast_to(tap_buf[pitch + b : pitch + b + 1, lanes], square)
        along = jnp.broadcast_to(tap_buf[2 * pitch + b : 2 * pitch + b + 1, lanes], square)
        for part, taps in ((0, plain + along * spread_y), (1, sideways)):
            rolled = pltpu.roll(taps, 0, 1, stride=1, stride_axis=0)
            high, low = split(jnp.where(band, rolled, 0.0))
            left[b, part * side : (part + 1) * side, lanes] = high
            left[b, (part + 2) * side : (part + 3) * side, lanes] = low


def put_block(block, b, side, images):
    high, low = split(block)
    images[b * side : (b + 1) * side, :side] = high
    images[b * side : (b + 1) * side, side:] = low


def across_stage(slots, side, images, across_high, across_low, right):
    for first in range(0, PROFILES, 2):
        last = min(first + 2, PROFILES)
        lanes = slice(first * side, last * side)
        high = across_high[:, lanes]
        doubled = jnp.concatenate([high, high], axis=0)
        result = mm(images[...], doubled) + mm(images[:, :side], across_low[:, lanes])
        for i in range(first, last):
            part_high, part_low = split(result[:, (i - first) * side : (i - first + 1) * side])
            for b in range(slots):
                rows = slice(i * side, (i + 1) * side)
                right[b, rows, :side] = part_high[b * side : (b + 1) * side]
                right[b, rows, side:] = part_low[b * side : (b + 1) * side]


def down_stage(b, side, left, right):
    result = mm(left[b], right[b])
    half = 2 * side
    both = result[:half, :side] + (result[:half, side:] + result[half:, :side])
    return both[:side] + both[side:] * spread_along((side, side), 1, side)


FIRST_FAR = 10


def fetch(sources, targets, semaphores):
    copies = [
        pltpu.make_async_copy(source, target, semaphores.at[n])
        for n, (source, target) in enumerate(zip(sources, targets, strict=True))
    ]
    for copy in copies:
        copy.start()

    def wait(*numbers):
        for n in numbers:
            copies[n].wait()

    return wait, targets


def first_kernel(
    slots, side, tiles, meta_blocks, visits,
    *refs,
):
    far, counts, keep, send = refs[:FIRST_FAR], *refs[FIRST_FAR : FIRST_FAR + 3]
    coef_buf, tap_buf, left, images, right, moved = refs[FIRST_FAR + 3 : FIRST_FAR + 9]
    wait, near = fetch(far, refs[FIRST_FAR + 9 : -1], refs[-1])
    coef, rows_high, rows_low, science, across_high, across_low = near[:6]
    weight, slot_tile, offsets, tile_place = near[6:]
    visit = lax.axis_index("visit")
    sky = lax.axis_index("sky")
    core = visit % 2
    peers = visits // 2
    share = side // visits
    wait(*range(FIRST_FAR))
    tap_rows(coef, coef_buf, tap_buf, rows_high, rows_low, slots)
    for b in range(slots):
        put_block(science[0, b], b, side, images)
        build_left(b, slots, side, tap_buf, left)
    across_stage(slots, side, images, across_high, across_low, right)
    first_lane = (visit * tiles + sky) * slots
    lane = lax.broadcasted_iota(jnp.int32, (META, LANES), 1)
    field = lax.broadcasted_iota(jnp.int32, (META, LANES), 0)
    meta = [jnp.zeros((META, LANES), F32) for _ in range(meta_blocks)]
    for b in range(slots):
        owner = tile_place[slot_tile[0, b]]
        usable = b < counts[0, 0]
        used = jnp.where(usable, weight[0, b], 0.0)
        top = offsets[0, 0, b]
        left_edge = offsets[0, 1, b]
        entry = jnp.where(
            field == 0,
            used,
            jnp.where(
                field == 1,
                top.astype(F32),
                jnp.where(field == 2, left_edge.astype(F32), jnp.where(field == 3, owner.astype(F32), 0.0)),
            ),
        )
        for m in range(meta_blocks):
            meta[m] = jnp.where(lane + m * LANES == first_lane + b, entry, meta[m])
        image = down_stage(b, side, left, right)
        image = jnp.where(usable, image * used, 0.0)
        moved[b] = pltpu.roll(image, left_edge, 1)
        for h, out in ((0, keep), (1, send)):

            def pick(q, b=b, h=h, out=out, top=top):
                residue = 2 * q + (core ^ h)
                start = first_row(top, residue, visits) * visits + residue - top
                out[pl.ds((q * slots + b) * share, share), :] = moved[
                    b, pl.ds(start, share, stride=visits), :
                ]

            repeat(peers, peers, pick)
    body = peers * slots * share
    for m in range(meta_blocks):
        keep[pl.ds(body + m * META, META), :] = meta[m]
        send[pl.ds(body + m * META, META), :] = meta[m]


def quotient(value, divisor):
    if divisor & (divisor - 1) == 0:
        return value >> (divisor.bit_length() - 1)
    return lax.div(value, divisor)


def repeat(count, width, step):
    if width <= 4:
        for n in range(count):
            step(n)
    else:
        lax.fori_loop(0, count, lambda n, carry: (step(n), carry)[1], 0)


def first_row(top, residue, visits):
    return quotient(top - residue + (visits - 1), visits)


def scatter_kernel(rows, peers, meta_rows, keep, received, *pieces):
    place = lax.axis_index("visit") // 2
    tail = pl.ds(peers * rows, meta_rows)
    meta = keep[tail, :] + received[tail, :]
    for j in range(peers):
        source = pl.ds((place ^ j) * rows, rows)
        pieces[j][pl.ds(0, rows), :] = keep[source, :]
        pieces[j][pl.ds(rows, rows), :] = received[source, :]
        pieces[j][pl.ds(2 * rows, meta_rows), :] = meta


def plane_kernel(slots, side, tiles, visits, meta_rows, *refs):
    peers = visits // 2
    share = side // visits
    size = 2 * (TILE // visits)
    sources, pieces = refs[:peers], refs[peers : peers + tiles]
    table, scalars, semaphore = refs[peers + tiles : peers + tiles + 3]
    sums = refs[peers + tiles + 3 :]
    visit = lax.axis_index("visit")
    sky = lax.axis_index("sky")
    core = visit % 2
    place = visit // 2
    tail = pl.ds(2 * slots * share, meta_rows)
    meta = sources[0][tail, :]
    for p in range(1, peers):
        meta = meta + sources[p][tail, :]
    table[...] = meta
    copy = pltpu.make_async_copy(table, scalars, semaphore)
    copy.start()
    for total in sums:
        total[...] = jnp.zeros(total.shape, F32)
    col = lax.broadcasted_iota(jnp.int32, (share, LANES), 1)
    copy.wait()

    def place_rows(h, b):
        for p in range(peers):
            total = sums[p % len(sums)]
            sender = 2 * (place ^ p) + (core ^ h)
            slot = (sender * tiles + sky) * slots + b
            base, lane = 0, slot
            if meta_rows > META:
                base = quotient(slot, LANES)
                lane = slot - base * LANES
                base = base * META
            top = scalars[base + 1, lane].astype(jnp.int32)
            left_edge = scalars[base + 2, lane].astype(jnp.int32)
            owner = scalars[base + 3, lane].astype(jnp.int32)
            rows = sources[p][pl.ds((h * slots + b) * share, share), :]
            where = pl.ds(first_row(top, visit, visits), share)
            total[owner, 0, where, :] += jnp.where(col >= left_edge, rows, 0.0)
            total[owner, 1, where, :] += jnp.where(col < left_edge, rows, 0.0)

    for h in range(2):
        repeat(slots, peers, lambda b, h=h: place_rows(h, b))
    for j in range(tiles):
        tile = sky ^ j
        for h in range(2):
            value = sums[0][tile, h]
            for total in sums[1:]:
                value = value + total[tile, h]
            pieces[j][pl.ds(h * (size // 2), size // 2), :] = value
        pieces[j][pl.ds(size, meta_rows), :] = meta


def template_kernel(tiles, strip, visits, meta_blocks, side, *refs):
    sources, out = refs[:tiles], refs[tiles]
    visit = lax.axis_index("visit")
    sky = lax.axis_index("sky")
    size = 2 * strip
    value = sources[0][...]
    for p in range(1, tiles):
        value = value + sources[p][...]
    y = (lax.broadcasted_iota(jnp.int32, (strip, LANES), 0) * visits + visit).astype(F32)
    x = lax.broadcasted_iota(jnp.int32, (TILE, LANES), 0).astype(F32)
    coverage = jnp.zeros((strip, TILE), F32)
    for m in range(meta_blocks):
        meta = value[size + m * META : size + (m + 1) * META]
        used, top, left, owner = meta[0:1], meta[1:2], meta[2:3], meta[3:4]
        inside = (y >= top) & (y < top + side) & (owner == sky.astype(F32))
        amount = jnp.where(inside, jnp.broadcast_to(used, y.shape), 0.0)
        columns = jnp.where((x >= left) & (x < left + side), 1.0, 0.0).astype(BF16)
        one, _ = split(amount)
        two = (amount - one.astype(F32)).astype(BF16)
        three = (amount - one.astype(F32) - two.astype(F32)).astype(BF16)
        for part in (one, two, three):
            coverage = coverage + lax.dot_general(
                part, columns, (((1,), (1,)), ((), ())), preferred_element_type=F32
            )
    for h in range(2):
        out[pl.ds(h * strip, strip), :] = value[h * strip : (h + 1) * strip] / (
            coverage[:, h * LANES : (h + 1) * LANES] + 1.0
        )


def stack_kernel(tiles, strip, *refs):
    sources, out = refs[:tiles], refs[tiles]
    size = 2 * strip
    for j in range(tiles):
        out[pl.ds(j * size, size), :] = sources[j][...]


def second_kernel(
    slots, side, tiles, strip, peers,
    left, across_high, across_low, science, counts, places,
    *refs,
):
    pieces, refs = refs[: 2 * peers], refs[2 * peers :]
    template, difference, images, right, total, staged, results, outward = refs
    visit = lax.axis_index("visit")
    sky = lax.axis_index("sky")
    core = visit % 2
    place = visit // 2
    for c in range(2):
        for j in range(peers):
            residue = 2 * (place ^ j) + (core ^ c)
            piece = pieces[c * peers + j]

            def spread_rows(t, residue=residue, piece=piece):
                for h in range(2):
                    total[sky ^ t, h, pl.ds(residue, strip, stride=2 * peers), :] = piece[
                        pl.ds((t * 2 + h) * strip, strip), :
                    ]

            repeat(tiles, peers, spread_rows)
    for h in range(2):
        staged[:, h * LANES : (h + 1) * LANES] = total[sky, h]
    copies = [pltpu.make_async_copy(staged, template.at[0], outward.at[slots])]
    copies[0].start()
    col = lax.broadcasted_iota(jnp.int32, (side, side), 1)
    for b in range(slots):
        owner, top, left_edge = places[0, b], places[1, b], places[2, b]
        joined = jnp.where(
            col >= left_edge, total[owner, 0, pl.ds(top, side), :], total[owner, 1, pl.ds(top, side), :]
        )
        put_block(pltpu.roll(joined, (side - left_edge) % side, 1), b, side, images)
    across_stage(slots, side, images, across_high, across_low, right)
    for b in range(slots):
        matched = down_stage(b, side, left, right)
        results[b] = jnp.where(b < counts[0, 0], science[0, b] - matched, 0.0)
        copies.append(pltpu.make_async_copy(results.at[b], difference.at[0, b], outward.at[b]))
        copies[-1].start()
    for copy in copies:
        copy.wait()


def prepare_kernel(
    slots, side, coef, rows_high, rows_low, slot_tile, offsets, tile_place, *refs,
):
    left, places = refs[3:5]
    coef_buf, tap_buf, semaphores = refs[8:]
    wait, _ = fetch(refs[:3], refs[5:8], semaphores)
    for b in range(slots):
        places[0, b] = tile_place[slot_tile[0, b]]
        places[1, b] = offsets[0, 0, b]
        places[2, b] = offsets[0, 1, b]
    tap_rows(coef, coef_buf, tap_buf, rows_high, rows_low, slots)
    for b in range(slots):
        build_left(b, slots, side, tap_buf, left)
    wait(0, 1, 2)


def body(science, coef_first, coef_second, weight, slot_tile, offsets, counts, tile_place):
    slots, side = science.shape[1], science.shape[2]
    basis = coef_first.shape[-1]
    visits = lax.axis_size("visit")
    tiles = lax.axis_size("sky")
    peers = visits // 2
    strip = TILE // visits
    rows = slots * (side // visits)
    meta_blocks = -(-visits * tiles * slots // LANES)
    meta_rows = meta_blocks * META
    across_high, across_low, rows_high, rows_low = (
        jnp.asarray(c) for c in constants(side, basis)
    )
    vmem = pl.BlockSpec(memory_space=pltpu.VMEM)
    smem = pl.BlockSpec(memory_space=pltpu.SMEM)
    anywhere = pl.BlockSpec(memory_space=pl.ANY)

    coef_first = coef_first.transpose(0, 2, 1, 3)
    coef_second = coef_second.transpose(0, 2, 1, 3)
    offsets = offsets.transpose(0, 2, 1)

    def shape(*dims):
        return pltpu.VMEM(dims, F32)

    def far(value):
        return pltpu.with_memory_space_constraint(value, pltpu.HBM)

    def near(value):
        return pltpu.with_memory_space_constraint(value, pltpu.VMEM)

    def call(function, ins, outs, specs=None, scratch=(), out_space=vmem):
        return pl.pallas_call(
            function,
            out_shape=outs,
            in_specs=specs or [vmem] * len(ins),
            out_specs=out_space
            if isinstance(out_space, list)
            else jax.tree.map(lambda _: out_space, outs),
            scratch_shapes=list(scratch),
            compiler_params=pltpu.CompilerParams(vmem_limit_bytes=VMEM_BYTES),
        )(*ins)

    tap_scratch = [
        pltpu.VMEM((-(-3 * row_pitch(slots) // 16) * 16, LANES), F32),
        pltpu.VMEM((-(-3 * row_pitch(slots) // 16) * 16, PROFILES * side), F32),
    ]
    left_shape = (slots, 4 * side, PROFILES * side)
    pass_scratch = [
        pltpu.VMEM((slots * side, 2 * side), BF16),
        pltpu.VMEM((slots, PROFILES * side, 2 * side), BF16),
        pltpu.VMEM((tiles, 2, TILE, LANES), F32),
    ]

    def flip(value, axis, size, mask):
        return lax.ppermute(value, axis, [(d, d ^ mask) for d in range(size)])

    def exchange(values, axis, size, step):
        out = [values[0]]
        for j in range(1, len(values)):
            out.append(flip(values[j], axis, size, step * j))
        return out

    first_far = (
        coef_first, rows_high, rows_low, science, across_high, across_low,
        weight, slot_tile, offsets, tile_place,
    )
    keep, send = call(
        lambda *refs: first_kernel(slots, side, tiles, meta_blocks, visits, *refs),
        (*map(far, first_far), counts),
        [shape(peers * rows + meta_rows, LANES)] * 2,
        specs=[anywhere] * FIRST_FAR + [smem],
        scratch=tap_scratch
        + [pltpu.VMEM(left_shape, BF16)]
        + pass_scratch[:2]
        + [pltpu.VMEM((slots, side, LANES), F32)]
        + [pltpu.VMEM(a.shape, a.dtype) for a in first_far[:6]]
        + [pltpu.SMEM(a.shape, a.dtype) for a in first_far[6:]]
        + [pltpu.SemaphoreType.DMA((FIRST_FAR,))],
    )
    ready = (across_high, across_low, science)
    left, places, *ready = call(
        lambda *refs: prepare_kernel(slots, side, *refs),
        tuple(
            map(far, (coef_second, rows_high, rows_low, slot_tile, offsets, tile_place, *ready))
        ),
        [pltpu.VMEM(left_shape, BF16), pltpu.SMEM((3, slots), jnp.int32)]
        + [pltpu.VMEM(a.shape, a.dtype) for a in ready],
        specs=[vmem] * 3 + [smem] * 3 + [anywhere] * 3,
        scratch=tap_scratch + [pltpu.SemaphoreType.DMA((3,))],
        out_space=[vmem, smem] + [vmem] * 3,
    )
    received = flip(send, "visit", visits, 1)
    pieces = call(
        lambda *refs: scatter_kernel(rows, peers, meta_rows, *refs),
        (near(keep), near(received)),
        [shape(2 * rows + meta_rows, LANES)] * peers,
    )
    arrived = exchange(pieces, "visit", visits, 2)
    pieces = call(
        lambda *refs: plane_kernel(slots, side, tiles, visits, meta_rows, *refs),
        [near(a) for a in arrived],
        [shape(2 * strip + meta_rows, LANES)] * tiles,
        scratch=[
            pltpu.VMEM((meta_rows, LANES), F32),
            pltpu.SMEM((meta_rows, LANES), F32),
            pltpu.SemaphoreType.DMA,
        ]
        + [pltpu.VMEM((tiles, 2, strip, LANES), F32)] * min(peers, 4),
    )
    arrived = exchange(pieces, "sky", tiles, 1)
    strip_own = call(
        lambda *refs: template_kernel(tiles, strip, visits, meta_blocks, side, *refs),
        [near(a) for a in arrived],
        shape(2 * strip, LANES),
    )
    strips = exchange([strip_own] * tiles, "sky", tiles, 1)
    piece = call(
        lambda *refs: stack_kernel(tiles, strip, *refs),
        [near(a) for a in strips],
        shape(tiles * 2 * strip, LANES),
    )
    mine = exchange([piece] * peers, "visit", visits, 2)
    theirs = [flip(p, "visit", visits, 1) for p in mine]
    template, difference = call(
        lambda *refs: second_kernel(slots, side, tiles, strip, peers, *refs),
        (near(left), *map(near, ready), counts,
         pltpu.with_memory_space_constraint(places, pltpu.SMEM),
         *map(near, mine), *map(near, theirs)),
        [jax.ShapeDtypeStruct(d, F32) for d in ((1, TILE, TILE), (1, slots, side, side))],
        specs=[vmem] * 4 + [smem] * 2 + [vmem] * (2 * peers),
        scratch=pass_scratch
        + [pltpu.VMEM((TILE, TILE), F32), pltpu.VMEM((slots, side, side), F32)]
        + [pltpu.SemaphoreType.DMA((slots + 1,))],
        out_space=anywhere,
    )
    return template, difference


def solution(mesh):
    in_specs = (
        P("visit", "sky", None, None),
        P("visit", "sky", None, None),
        P("visit", "sky", None, None),
        P("visit", "sky"),
        P("visit", "sky"),
        P("visit", "sky", None),
        P("visit", "sky"),
        P(),
    )
    out_specs = (P("sky", None, None), P("visit", "sky", None, None))

    return jax.shard_map(body, mesh=mesh, in_specs=in_specs, out_specs=out_specs, check_vma=False)
```

```python
import numpy as np
import jax
import jax.numpy as jnp
from jax import lax
from jax.experimental import pallas as pl
from jax.experimental.pallas import tpu as pltpu
from jax.sharding import PartitionSpec as P


TILE = 256
TAPS = 21
PROFILES = 7
WIDTHS = (1.0, 1.0, 1.0, 2.5, 2.5, 2.5, 5.0)
POWERS = (0, 1, 2, 0, 1, 2, 0)
LANES = 128
META = 8
VMEM_BYTES = 24 * 2**20


F32 = jnp.float32
BF16 = jnp.bfloat16


def split_np(values):
    values = np.asarray(values, np.float32)
    high = values.astype(BF16)
    low = (values - high.astype(np.float32)).astype(BF16)
    return high, low


def constants(side, basis):
    reach = (TAPS - 1) // 2
    support = np.arange(TAPS).astype(np.float64) - reach
    taps = []
    for number in range(PROFILES):
        sample = support ** POWERS[number] * np.exp(
            -support * support / (2.0 * WIDTHS[number] ** 2)
        )
        taps.append(sample / np.sqrt(np.sum(sample * sample)))
    taps = np.stack(taps)
    places = np.arange(side)
    spacing = places[:, None] - places[None, :]
    inside = np.abs(spacing) <= reach
    across = np.concatenate(
        [np.where(inside, t[np.clip(spacing + reach, 0, TAPS - 1)], 0.0) for t in taps], axis=1
    )
    rows = np.zeros((-(-basis // 64) * 64, PROFILES * side), np.float64)
    for i in range(PROFILES):
        for j in range(PROFILES):
            for t in range(-reach, reach + 1):
                rows[PROFILES * i + j, i * side + t % side] = taps[j, t + reach]
    return split_np(across) + split_np(rows)


def row_pitch(slots):
    return -(-slots // 8) * 8


def split(values):
    high = values.astype(BF16)
    low = (values - high.astype(F32)).astype(BF16)
    return high, low


def mm(a, b):
    return jnp.dot(a, b, preferred_element_type=F32)


def spread_along(shape, axis, side):
    places = lax.broadcasted_iota(jnp.int32, shape, axis).astype(F32)
    return (2.0 * places - (side - 1)) / (side - 1)


def tap_rows(coef_ref, coef_buf, tap_buf, rows_high, rows_low, slots):
    coef_buf[...] = jnp.zeros(coef_buf.shape, F32)
    basis = coef_ref.shape[-1]
    depth = rows_high.shape[0]
    pitch = row_pitch(slots)
    rows = coef_buf.shape[0]
    for k in range(3):
        coef_buf[pl.ds(pitch * k, slots), pl.ds(0, basis)] = coef_ref[0, k]
    high, low = split(coef_buf[:, :depth])
    both = mm(jnp.concatenate([high, low], axis=0), rows_high[...])
    tap_buf[...] = both[:rows] + (both[rows:] + mm(high, rows_low[...]))


def build_left(b, slots, side, tap_buf, left):
    reach = (TAPS - 1) // 2
    square = (side, side)
    row = lax.broadcasted_iota(jnp.int32, square, 0)
    col = lax.broadcasted_iota(jnp.int32, square, 1)
    band = jnp.abs(col - row) <= reach
    spread_y = spread_along(square, 0, side)
    pitch = row_pitch(slots)
    for i in range(PROFILES):
        lanes = slice(i * side, (i + 1) * side)
        plain = jnp.broadcast_to(tap_buf[b : b + 1, lanes], square)
        sideways = jnp.broadcast_to(tap_buf[pitch + b : pitch + b + 1, lanes], square)
        along = jnp.broadcast_to(tap_buf[2 * pitch + b : 2 * pitch + b + 1, lanes], square)
        for part, taps in ((0, plain + along * spread_y), (1, sideways)):
            rolled = pltpu.roll(taps, 0, 1, stride=1, stride_axis=0)
            high, low = split(jnp.where(band, rolled, 0.0))
            left[b, part * side : (part + 1) * side, lanes] = high
            left[b, (part + 2) * side : (part + 3) * side, lanes] = low


def put_block(block, b, side, images):
    high, low = split(block)
    images[b * side : (b + 1) * side, :side] = high
    images[b * side : (b + 1) * side, side:] = low


def across_stage(slots, side, images, across_high, across_low, right):
    for first in range(0, PROFILES, 2):
        last = min(first + 2, PROFILES)
        lanes = slice(first * side, last * side)
        high = across_high[:, lanes]
        doubled = jnp.concatenate([high, high], axis=0)
        result = mm(images[...], doubled) + mm(images[:, :side], across_low[:, lanes])
        for i in range(first, last):
            part_high, part_low = split(result[:, (i - first) * side : (i - first + 1) * side])
            for b in range(slots):
                rows = slice(i * side, (i + 1) * side)
                right[b, rows, :side] = part_high[b * side : (b + 1) * side]
                right[b, rows, side:] = part_low[b * side : (b + 1) * side]


def down_stage(b, side, left, right):
    result = mm(left[b], right[b])
    half = 2 * side
    both = result[:half, :side] + (result[:half, side:] + result[half:, :side])
    return both[:side] + both[side:] * spread_along((side, side), 1, side)


FIRST_FAR = 10


def fetch(sources, targets, semaphores):
    copies = [
        pltpu.make_async_copy(source, target, semaphores.at[n])
        for n, (source, target) in enumerate(zip(sources, targets, strict=True))
    ]
    for copy in copies:
        copy.start()

    def wait(*numbers):
        for n in numbers:
            copies[n].wait()

    return wait, targets


def first_kernel(
    slots, side, tiles, meta_blocks, visits,
    *refs,
):
    far, counts, keep, send = refs[:FIRST_FAR], *refs[FIRST_FAR : FIRST_FAR + 3]
    coef_buf, tap_buf, left, images, right, moved = refs[FIRST_FAR + 3 : FIRST_FAR + 9]
    wait, near = fetch(far, refs[FIRST_FAR + 9 : -1], refs[-1])
    coef, rows_high, rows_low, science, across_high, across_low = near[:6]
    weight, slot_tile, offsets, tile_place = near[6:]
    visit = lax.axis_index("visit")
    sky = lax.axis_index("sky")
    core = visit % 2
    peers = visits // 2
    share = side // visits
    wait(0, 1, 2)
    tap_rows(coef, coef_buf, tap_buf, rows_high, rows_low, slots)
    wait(*range(3, FIRST_FAR))
    for b in range(slots):
        put_block(science[0, b], b, side, images)
        build_left(b, slots, side, tap_buf, left)
    across_stage(slots, side, images, across_high, across_low, right)
    first_lane = (visit * tiles + sky) * slots
    lane = lax.broadcasted_iota(jnp.int32, (META, LANES), 1)
    field = lax.broadcasted_iota(jnp.int32, (META, LANES), 0)
    meta = [jnp.zeros((META, LANES), F32) for _ in range(meta_blocks)]
    for b in range(slots):
        owner = tile_place[slot_tile[0, b]]
        usable = b < counts[0, 0]
        used = jnp.where(usable, weight[0, b], 0.0)
        top = offsets[0, 0, b]
        left_edge = offsets[0, 1, b]
        entry = jnp.where(
            field == 0,
            used,
            jnp.where(
                field == 1,
                top.astype(F32),
                jnp.where(field == 2, left_edge.astype(F32), jnp.where(field == 3, owner.astype(F32), 0.0)),
            ),
        )
        for m in range(meta_blocks):
            meta[m] = jnp.where(lane + m * LANES == first_lane + b, entry, meta[m])
        image = down_stage(b, side, left, right)
        image = jnp.where(usable, image * used, 0.0)
        moved[b] = pltpu.roll(image, left_edge, 1)
        for h, out in ((0, keep), (1, send)):

            def pick(q, b=b, h=h, out=out, top=top):
                residue = 2 * q + (core ^ h)
                start = first_row(top, residue, visits) * visits + residue - top
                out[pl.ds((q * slots + b) * share, share), :] = moved[
                    b, pl.ds(start, share, stride=visits), :
                ]

            repeat(peers, peers, pick)
    body = peers * slots * share
    for m in range(meta_blocks):
        keep[pl.ds(body + m * META, META), :] = meta[m]
        send[pl.ds(body + m * META, META), :] = meta[m]


def quotient(value, divisor):
    if divisor & (divisor - 1) == 0:
        return value >> (divisor.bit_length() - 1)
    return lax.div(value, divisor)


def repeat(count, width, step):
    if width <= 4:
        for n in range(count):
            step(n)
    else:
        lax.fori_loop(0, count, lambda n, carry: (step(n), carry)[1], 0)


def first_row(top, residue, visits):
    return quotient(top - residue + (visits - 1), visits)


def scatter_kernel(rows, peers, meta_rows, keep, received, *pieces):
    place = lax.axis_index("visit") // 2
    tail = pl.ds(peers * rows, meta_rows)
    meta = keep[tail, :] + received[tail, :]
    for j in range(peers):
        source = pl.ds((place ^ j) * rows, rows)
        pieces[j][pl.ds(0, rows), :] = keep[source, :]
        pieces[j][pl.ds(rows, rows), :] = received[source, :]
        pieces[j][pl.ds(2 * rows, meta_rows), :] = meta


def look_up(scalars, slot):
    base, lane = 0, slot
    if scalars.shape[0] > META:
        base = quotient(slot, LANES)
        lane = slot - base * LANES
        base = base * META
    return tuple(scalars[base + n, lane].astype(jnp.int32) for n in (1, 2, 3))


def plane_kernel(slots, side, tiles, visits, meta_rows, *refs):
    peers = visits // 2
    share = side // visits
    size = 2 * (TILE // visits)
    sources, pieces = refs[:peers], refs[peers : peers + tiles]
    scalars, table, semaphore = refs[peers + tiles : peers + tiles + 3]
    sums = refs[peers + tiles + 3 :]
    visit = lax.axis_index("visit")
    sky = lax.axis_index("sky")
    core = visit % 2
    place = visit // 2
    tail = pl.ds(2 * slots * share, meta_rows)
    meta = sources[0][tail, :]
    for p in range(1, peers):
        meta = meta + sources[p][tail, :]
    table[...] = meta
    copy = pltpu.make_async_copy(table, scalars, semaphore)
    copy.start()
    for total in sums:
        total[...] = jnp.zeros(total.shape, F32)
    col = lax.broadcasted_iota(jnp.int32, (share, LANES), 1)
    copy.wait()

    def place_rows(h, b):
        for p in range(peers):
            total = sums[p % len(sums)]
            sender = 2 * (place ^ p) + (core ^ h)
            top, left_edge, owner = look_up(scalars, (sender * tiles + sky) * slots + b)
            rows = sources[p][pl.ds((h * slots + b) * share, share), :]
            where = pl.ds(first_row(top, visit, visits), share)
            total[owner, 0, where, :] += jnp.where(col >= left_edge, rows, 0.0)
            total[owner, 1, where, :] += jnp.where(col < left_edge, rows, 0.0)

    for h in range(2):
        repeat(slots, peers, lambda b, h=h: place_rows(h, b))
    for j in range(tiles):
        tile = sky ^ j
        for h in range(2):
            value = sums[0][tile, h]
            for total in sums[1:]:
                value = value + total[tile, h]
            pieces[j][pl.ds(h * (size // 2), size // 2), :] = value
        pieces[j][pl.ds(size, meta_rows), :] = meta


def template_kernel(tiles, strip, visits, meta_blocks, side, *refs):
    sources, out = refs[:tiles], refs[tiles]
    visit = lax.axis_index("visit")
    sky = lax.axis_index("sky")
    size = 2 * strip
    value = sources[0][...]
    for p in range(1, tiles):
        value = value + sources[p][...]
    y = (lax.broadcasted_iota(jnp.int32, (strip, LANES), 0) * visits + visit).astype(F32)
    x = lax.broadcasted_iota(jnp.int32, (TILE, LANES), 0).astype(F32)
    coverage = jnp.zeros((strip, TILE), F32)
    for m in range(meta_blocks):
        meta = value[size + m * META : size + (m + 1) * META]
        used, top, left, owner = meta[0:1], meta[1:2], meta[2:3], meta[3:4]
        inside = (y >= top) & (y < top + side) & (owner == sky.astype(F32))
        amount = jnp.where(inside, jnp.broadcast_to(used, y.shape), 0.0)
        columns = jnp.where((x >= left) & (x < left + side), 1.0, 0.0).astype(BF16)
        one, _ = split(amount)
        two = (amount - one.astype(F32)).astype(BF16)
        three = (amount - one.astype(F32) - two.astype(F32)).astype(BF16)
        for part in (one, two, three):
            coverage = coverage + lax.dot_general(
                part, columns, (((1,), (1,)), ((), ())), preferred_element_type=F32
            )
    for h in range(2):
        out[pl.ds(h * strip, strip), :] = value[h * strip : (h + 1) * strip] / (
            coverage[:, h * LANES : (h + 1) * LANES] + 1.0
        )


def hold_kernel(source, out):
    out[...] = source[pl.ds(0, META), :]


def select_kernel(slots, side, tiles, visits, scalars, *refs):
    peers = visits // 2
    share = side // visits
    strip = TILE // visits
    sources, pieces, tile_rows = refs[:tiles], refs[tiles : tiles + peers], refs[tiles + peers]
    visit = lax.axis_index("visit")
    sky = lax.axis_index("sky")
    core = visit % 2
    place = visit // 2
    for j in range(tiles):
        for h in range(2):
            tile_rows[sky ^ j, h] = sources[j][pl.ds(h * strip, strip), :]
    col = lax.broadcasted_iota(jnp.int32, (share, LANES), 1)
    for j in range(peers):
        piece = pieces[j]
        piece[pl.ds(2 * slots * share, 2 * strip), :] = sources[0][...]

        def pick(n, j=j, piece=piece):
            h, b = quotient(n, slots), n % slots
            reader = 2 * (place ^ j) + (core ^ h)
            top, left_edge, owner = look_up(scalars, (reader * tiles + sky) * slots + b)
            where = pl.ds(first_row(top, visit, visits), share)
            piece[pl.ds(n * share, share), :] = jnp.where(
                col >= left_edge, tile_rows[owner, 0, where, :], tile_rows[owner, 1, where, :]
            )

        repeat(2 * slots, peers, pick)


def second_kernel(
    slots, side, strip, peers,
    left, across_high, across_low, science, counts, places,
    *refs,
):
    pieces, refs = refs[: 2 * peers], refs[2 * peers :]
    template, difference, images, right, total, windows, staged, results, outward = refs[-9:]
    visits = 2 * peers
    share = side // visits
    visit = lax.axis_index("visit")
    core = visit % 2
    place = visit // 2
    for c in range(2):
        for j in range(peers):
            residue = 2 * (place ^ j) + (core ^ c)
            piece = pieces[c * peers + j]

            for h in range(2):
                total[h, pl.ds(residue, strip, stride=visits), :] = piece[
                    pl.ds(2 * slots * share + h * strip, strip), :
                ]

            def spread_rows(b, c=c, residue=residue, piece=piece):
                top = places[1, b]
                start = first_row(top, residue, visits) * visits + residue - top
                windows[b, pl.ds(start, share, stride=visits), :] = piece[
                    pl.ds((c * slots + b) * share, share), :
                ]

            repeat(slots, peers, spread_rows)
    for h in range(2):
        staged[:, h * LANES : (h + 1) * LANES] = total[h]
    copies = [pltpu.make_async_copy(staged, template.at[0], outward.at[slots])]
    copies[0].start()
    for b in range(slots):
        block = pltpu.roll(windows[b], (side - places[2, b]) % side, 1)
        put_block(block, b, side, images)
    across_stage(slots, side, images, across_high, across_low, right)
    for b in range(slots):
        matched = down_stage(b, side, left, right)
        results[b] = jnp.where(b < counts[0, 0], science[0, b] - matched, 0.0)
        copies.append(pltpu.make_async_copy(results.at[b], difference.at[0, b], outward.at[b]))
        copies[-1].start()
    for copy in copies:
        copy.wait()


def prepare_kernel(
    slots, side, coef, rows_high, rows_low, slot_tile, offsets, tile_place, *refs,
):
    left, places = refs[3:5]
    coef_buf, tap_buf, semaphores = refs[8:]
    wait, _ = fetch(refs[:3], refs[5:8], semaphores)
    for b in range(slots):
        places[0, b] = tile_place[slot_tile[0, b]]
        places[1, b] = offsets[0, 0, b]
        places[2, b] = offsets[0, 1, b]
    tap_rows(coef, coef_buf, tap_buf, rows_high, rows_low, slots)
    for b in range(slots):
        build_left(b, slots, side, tap_buf, left)
    wait(0, 1, 2)


def body(science, coef_first, coef_second, weight, slot_tile, offsets, counts, tile_place):
    slots, side = science.shape[1], science.shape[2]
    basis = coef_first.shape[-1]
    visits = lax.axis_size("visit")
    tiles = lax.axis_size("sky")
    peers = visits // 2
    strip = TILE // visits
    rows = slots * (side // visits)
    meta_blocks = -(-visits * tiles * slots // LANES)
    meta_rows = meta_blocks * META
    across_high, across_low, rows_high, rows_low = (
        jnp.asarray(c) for c in constants(side, basis)
    )
    vmem = pl.BlockSpec(memory_space=pltpu.VMEM)
    smem = pl.BlockSpec(memory_space=pltpu.SMEM)
    anywhere = pl.BlockSpec(memory_space=pl.ANY)

    coef_first = coef_first.transpose(0, 2, 1, 3)
    coef_second = coef_second.transpose(0, 2, 1, 3)
    offsets = offsets.transpose(0, 2, 1)

    def shape(*dims):
        return pltpu.VMEM(dims, F32)

    def far(value):
        return pltpu.with_memory_space_constraint(value, pltpu.HBM)

    def near(value):
        return pltpu.with_memory_space_constraint(value, pltpu.VMEM)

    def call(function, ins, outs, specs=None, scratch=(), out_space=vmem):
        return pl.pallas_call(
            function,
            out_shape=outs,
            in_specs=specs or [vmem] * len(ins),
            out_specs=out_space
            if isinstance(out_space, list)
            else jax.tree.map(lambda _: out_space, outs),
            scratch_shapes=list(scratch),
            compiler_params=pltpu.CompilerParams(vmem_limit_bytes=VMEM_BYTES),
        )(*ins)

    tap_scratch = [
        pltpu.VMEM((-(-3 * row_pitch(slots) // 16) * 16, LANES), F32),
        pltpu.VMEM((-(-3 * row_pitch(slots) // 16) * 16, PROFILES * side), F32),
    ]
    left_shape = (slots, 4 * side, PROFILES * side)
    pass_scratch = [
        pltpu.VMEM((slots * side, 2 * side), BF16),
        pltpu.VMEM((slots, PROFILES * side, 2 * side), BF16),
        pltpu.VMEM((2, TILE, LANES), F32),
        pltpu.VMEM((slots, side, LANES), F32),
    ]

    def flip(value, axis, size, mask):
        return lax.ppermute(value, axis, [(d, d ^ mask) for d in range(size)])

    def exchange(values, axis, size, step):
        out = [values[0]]
        for j in range(1, len(values)):
            out.append(flip(values[j], axis, size, step * j))
        return out

    first_far = (
        coef_first, rows_high, rows_low, science, across_high, across_low,
        weight, slot_tile, offsets, tile_place,
    )
    keep, send = call(
        lambda *refs: first_kernel(slots, side, tiles, meta_blocks, visits, *refs),
        (*map(far, first_far), counts),
        [shape(peers * rows + meta_rows, LANES)] * 2,
        specs=[anywhere] * FIRST_FAR + [smem],
        scratch=tap_scratch
        + [pltpu.VMEM(left_shape, BF16)]
        + pass_scratch[:2]
        + [pltpu.VMEM((slots, side, LANES), F32)]
        + [pltpu.VMEM(a.shape, a.dtype) for a in first_far[:6]]
        + [pltpu.SMEM(a.shape, a.dtype) for a in first_far[6:]]
        + [pltpu.SemaphoreType.DMA((FIRST_FAR,))],
    )
    ready = (across_high, across_low, science)
    left, places, *ready = call(
        lambda *refs: prepare_kernel(slots, side, *refs),
        tuple(
            map(far, (coef_second, rows_high, rows_low, slot_tile, offsets, tile_place, *ready))
        ),
        [pltpu.VMEM(left_shape, BF16), pltpu.SMEM((3, slots), jnp.int32)]
        + [pltpu.VMEM(a.shape, a.dtype) for a in ready],
        specs=[vmem] * 3 + [smem] * 3 + [anywhere] * 3,
        scratch=tap_scratch + [pltpu.SemaphoreType.DMA((3,))],
        out_space=[vmem, smem] + [vmem] * 3,
    )
    received = flip(send, "visit", visits, 1)
    pieces = call(
        lambda *refs: scatter_kernel(rows, peers, meta_rows, *refs),
        (near(keep), near(received)),
        [shape(2 * rows + meta_rows, LANES)] * peers,
    )
    arrived = exchange(pieces, "visit", visits, 2)
    *pieces, scalars = call(
        lambda *refs: plane_kernel(slots, side, tiles, visits, meta_rows, *refs),
        [near(a) for a in arrived],
        [shape(2 * strip + meta_rows, LANES)] * tiles + [pltpu.SMEM((meta_rows, LANES), F32)],
        out_space=[vmem] * tiles + [smem],
        scratch=[pltpu.VMEM((meta_rows, LANES), F32), pltpu.SemaphoreType.DMA]
        + [pltpu.VMEM((tiles, 2, strip, LANES), F32)] * min(peers, 4),
    )
    arrived = exchange(pieces, "sky", tiles, 1)
    strip_own = call(
        lambda *refs: template_kernel(tiles, strip, visits, meta_blocks, side, *refs),
        [near(a) for a in arrived],
        shape(2 * strip, LANES),
    )
    strips = exchange([strip_own] * tiles, "sky", tiles, 1)
    pieces = call(
        lambda *refs: select_kernel(slots, side, tiles, visits, *refs),
        (pltpu.with_memory_space_constraint(scalars, pltpu.SMEM), *map(near, strips)),
        [shape(2 * strip + 2 * rows, LANES)] * peers,
        specs=[smem] + [vmem] * tiles,
        scratch=[pltpu.VMEM((tiles, 2, strip, LANES), F32)],
    )
    mine = exchange(pieces, "visit", visits, 2)
    theirs, markers = [], []
    for j in range(peers):
        theirs.append(flip(mine[j], "visit", visits, 1))
        if j > 1:
            markers.append(call(hold_kernel, (near(mine[j]),), shape(META, LANES)))
    template, difference = call(
        lambda *refs: second_kernel(slots, side, strip, peers, *refs),
        (near(left), *map(near, ready), counts,
         pltpu.with_memory_space_constraint(places, pltpu.SMEM),
         *map(near, mine), *map(near, theirs), *map(near, markers)),
        [jax.ShapeDtypeStruct(d, F32) for d in ((1, TILE, TILE), (1, slots, side, side))],
        specs=[vmem] * 4 + [smem] * 2 + [vmem] * (2 * peers + len(markers)),
        scratch=pass_scratch
        + [pltpu.VMEM((TILE, TILE), F32), pltpu.VMEM((slots, side, side), F32)]
        + [pltpu.SemaphoreType.DMA((slots + 1,))],
        out_space=anywhere,
    )
    return template, difference


def solution(mesh):
    in_specs = (
        P("visit", "sky", None, None),
        P("visit", "sky", None, None),
        P("visit", "sky", None, None),
        P("visit", "sky"),
        P("visit", "sky"),
        P("visit", "sky", None),
        P("visit", "sky"),
        P(),
    )
    out_specs = (P("sky", None, None), P("visit", "sky", None, None))

    return jax.shard_map(body, mesh=mesh, in_specs=in_specs, out_specs=out_specs, check_vma=False)
```

```python
import numpy as np
import jax
import jax.numpy as jnp
from jax import lax
from jax.experimental import pallas as pl
from jax.experimental.pallas import tpu as pltpu
from jax.sharding import PartitionSpec as P


TILE = 256
TAPS = 21
PROFILES = 7
WIDTHS = (1.0, 1.0, 1.0, 2.5, 2.5, 2.5, 5.0)
POWERS = (0, 1, 2, 0, 1, 2, 0)
LANES = 128
META = 8
VMEM_BYTES = 24 * 2**20


F32 = jnp.float32
BF16 = jnp.bfloat16


def split_np(values):
    values = np.asarray(values, np.float32)
    high = values.astype(BF16)
    low = (values - high.astype(np.float32)).astype(BF16)
    return high, low


def constants(side, basis):
    reach = (TAPS - 1) // 2
    support = np.arange(TAPS).astype(np.float64) - reach
    taps = []
    for number in range(PROFILES):
        sample = support ** POWERS[number] * np.exp(
            -support * support / (2.0 * WIDTHS[number] ** 2)
        )
        taps.append(sample / np.sqrt(np.sum(sample * sample)))
    taps = np.stack(taps)
    places = np.arange(side)
    spacing = places[:, None] - places[None, :]
    inside = np.abs(spacing) <= reach
    across = np.concatenate(
        [np.where(inside, t[np.clip(spacing + reach, 0, TAPS - 1)], 0.0) for t in taps], axis=1
    )
    rows = np.zeros((-(-basis // 64) * 64, PROFILES * side), np.float64)
    for i in range(PROFILES):
        for j in range(PROFILES):
            for t in range(-reach, reach + 1):
                rows[PROFILES * i + j, i * side + t % side] = taps[j, t + reach]
    return split_np(across) + split_np(rows)


def row_pitch(slots):
    return -(-slots // 8) * 8


def split(values):
    high = values.astype(BF16)
    low = (values - high.astype(F32)).astype(BF16)
    return high, low


def mm(a, b):
    return jnp.dot(a, b, preferred_element_type=F32)


def spread_along(shape, axis, side):
    places = lax.broadcasted_iota(jnp.int32, shape, axis).astype(F32)
    return (2.0 * places - (side - 1)) / (side - 1)


def tap_rows(coef_ref, coef_buf, tap_buf, rows_high, rows_low, slots):
    coef_buf[...] = jnp.zeros(coef_buf.shape, F32)
    basis = coef_ref.shape[-1]
    depth = rows_high.shape[0]
    pitch = row_pitch(slots)
    rows = coef_buf.shape[0]
    for k in range(3):
        coef_buf[pl.ds(pitch * k, slots), pl.ds(0, basis)] = coef_ref[0, k]
    high, low = split(coef_buf[:, :depth])
    both = mm(jnp.concatenate([high, low], axis=0), rows_high[...])
    tap_buf[...] = both[:rows] + (both[rows:] + mm(high, rows_low[...]))


def build_left(b, slots, side, tap_buf, left):
    reach = (TAPS - 1) // 2
    square = (side, side)
    row = lax.broadcasted_iota(jnp.int32, square, 0)
    col = lax.broadcasted_iota(jnp.int32, square, 1)
    band = jnp.abs(col - row) <= reach
    spread_y = spread_along(square, 0, side)
    pitch = row_pitch(slots)
    for i in range(PROFILES):
        lanes = slice(i * side, (i + 1) * side)
        plain = jnp.broadcast_to(tap_buf[b : b + 1, lanes], square)
        sideways = jnp.broadcast_to(tap_buf[pitch + b : pitch + b + 1, lanes], square)
        along = jnp.broadcast_to(tap_buf[2 * pitch + b : 2 * pitch + b + 1, lanes], square)
        for part, taps in ((0, plain + along * spread_y), (1, sideways)):
            rolled = pltpu.roll(taps, 0, 1, stride=1, stride_axis=0)
            high, low = split(jnp.where(band, rolled, 0.0))
            left[b, part * side : (part + 1) * side, lanes] = high
            left[b, (part + 2) * side : (part + 3) * side, lanes] = low


def put_block(block, b, side, images):
    high, low = split(block)
    images[b * side : (b + 1) * side, :side] = high
    images[b * side : (b + 1) * side, side:] = low


def across_stage(slots, side, images, across_high, across_low, right):
    for first in range(0, PROFILES, 2):
        last = min(first + 2, PROFILES)
        lanes = slice(first * side, last * side)
        high = across_high[:, lanes]
        doubled = jnp.concatenate([high, high], axis=0)
        result = mm(images[...], doubled) + mm(images[:, :side], across_low[:, lanes])
        for i in range(first, last):
            part_high, part_low = split(result[:, (i - first) * side : (i - first + 1) * side])
            for b in range(slots):
                rows = slice(i * side, (i + 1) * side)
                right[b, rows, :side] = part_high[b * side : (b + 1) * side]
                right[b, rows, side:] = part_low[b * side : (b + 1) * side]


def down_stage(b, side, left, right):
    result = mm(left[b], right[b])
    half = 2 * side
    both = result[:half, :side] + (result[:half, side:] + result[half:, :side])
    return both[:side] + both[side:] * spread_along((side, side), 1, side)


FIRST_FAR = 10


def fetch(sources, targets, semaphores):
    copies = [
        pltpu.make_async_copy(source, target, semaphores.at[n])
        for n, (source, target) in enumerate(zip(sources, targets, strict=True))
    ]
    for copy in copies:
        copy.start()

    def wait(*numbers):
        for n in numbers:
            copies[n].wait()

    return wait, targets


def first_kernel(
    slots, side, tiles, meta_blocks, visits,
    *refs,
):
    far, counts, keep, send = refs[:FIRST_FAR], *refs[FIRST_FAR : FIRST_FAR + 3]
    coef_buf, tap_buf, left, images, right, moved = refs[FIRST_FAR + 3 : FIRST_FAR + 9]
    wait, near = fetch(far, refs[FIRST_FAR + 9 : -1], refs[-1])
    coef, rows_high, rows_low, science, across_high, across_low = near[:6]
    weight, slot_tile, offsets, tile_place = near[6:]
    visit = lax.axis_index("visit")
    sky = lax.axis_index("sky")
    core = visit % 2
    peers = visits // 2
    share = side // visits
    wait(0, 1, 2)
    tap_rows(coef, coef_buf, tap_buf, rows_high, rows_low, slots)
    wait(*range(3, FIRST_FAR))
    for b in range(slots):
        put_block(science[0, b], b, side, images)
        build_left(b, slots, side, tap_buf, left)
    across_stage(slots, side, images, across_high, across_low, right)
    first_lane = (visit * tiles + sky) * slots
    lane = lax.broadcasted_iota(jnp.int32, (META, LANES), 1)
    field = lax.broadcasted_iota(jnp.int32, (META, LANES), 0)
    meta = [jnp.zeros((META, LANES), F32) for _ in range(meta_blocks)]
    for b in range(slots):
        owner = tile_place[slot_tile[0, b]]
        usable = b < counts[0, 0]
        used = jnp.where(usable, weight[0, b], 0.0)
        top = offsets[0, 0, b]
        left_edge = offsets[0, 1, b]
        entry = jnp.where(
            field == 0,
            used,
            jnp.where(
                field == 1,
                top.astype(F32),
                jnp.where(field == 2, left_edge.astype(F32), jnp.where(field == 3, owner.astype(F32), 0.0)),
            ),
        )
        for m in range(meta_blocks):
            meta[m] = jnp.where(lane + m * LANES == first_lane + b, entry, meta[m])
        image = down_stage(b, side, left, right)
        image = jnp.where(usable, image * used, 0.0)
        moved[b] = pltpu.roll(image, left_edge, 1)
        for h, out in ((0, keep), (1, send)):

            def pick(q, b=b, h=h, out=out, top=top):
                residue = 2 * q + (core ^ h)
                start = first_row(top, residue, visits) * visits + residue - top
                out[pl.ds((q * slots + b) * share, share), :] = moved[
                    b, pl.ds(start, share, stride=visits), :
                ]

            repeat(peers, peers, pick)
    body = peers * slots * share
    for m in range(meta_blocks):
        keep[pl.ds(body + m * META, META), :] = meta[m]
        send[pl.ds(body + m * META, META), :] = meta[m]


def quotient(value, divisor):
    if divisor & (divisor - 1) == 0:
        return value >> (divisor.bit_length() - 1)
    return lax.div(value, divisor)


def repeat(count, width, step):
    if width <= 4:
        for n in range(count):
            step(n)
    else:
        lax.fori_loop(0, count, lambda n, carry: (step(n), carry)[1], 0)


def first_row(top, residue, visits):
    return quotient(top - residue + (visits - 1), visits)


def scatter_kernel(rows, peers, meta_rows, keep, received, *pieces):
    place = lax.axis_index("visit") // 2
    tail = pl.ds(peers * rows, meta_rows)
    meta = keep[tail, :] + received[tail, :]
    for j in range(peers):
        source = pl.ds((place ^ j) * rows, rows)
        pieces[j][pl.ds(0, rows), :] = keep[source, :]
        pieces[j][pl.ds(rows, rows), :] = received[source, :]
        pieces[j][pl.ds(2 * rows, meta_rows), :] = meta


def look_up(scalars, slot):
    base, lane = 0, slot
    if scalars.shape[0] > META:
        base = quotient(slot, LANES)
        lane = slot - base * LANES
        base = base * META
    code = scalars[base, lane]
    return code >> 8, code & 255


def plane_kernel(slots, side, tiles, visits, meta_rows, *refs):
    peers = visits // 2
    share = side // visits
    strip = TILE // visits
    size = 2 * strip
    sources, pieces = refs[:peers], refs[peers : peers + tiles]
    scalars, table, semaphore = refs[peers + tiles : peers + tiles + 3]
    sums = refs[peers + tiles + 3 :]
    visit = lax.axis_index("visit")
    sky = lax.axis_index("sky")
    core = visit % 2
    place = visit // 2
    tail = pl.ds(2 * slots * share, meta_rows)
    meta = sources[0][tail, :]
    for p in range(1, peers):
        meta = meta + sources[p][tail, :]
    for m in range(meta_rows // META):
        top, left_edge, owner = (
            meta[m * META + n : m * META + n + 1].astype(jnp.int32) for n in (1, 2, 3)
        )
        row = owner * size + first_row(top, visit, visits)
        table[m * META : (m + 1) * META, :] = jnp.broadcast_to(
            (row << 8) + left_edge, (META, LANES)
        )
    copy = pltpu.make_async_copy(table, scalars, semaphore)
    copy.start()
    for total in sums:
        total[...] = jnp.zeros(total.shape, F32)
    col = lax.broadcasted_iota(jnp.int32, (share, LANES), 1)
    copy.wait()

    def place_rows(h, b):
        for p in range(peers):
            total = sums[p % len(sums)]
            sender = 2 * (place ^ p) + (core ^ h)
            row, left_edge = look_up(scalars, (sender * tiles + sky) * slots + b)
            rows = sources[p][pl.ds((h * slots + b) * share, share), :]
            total[pl.ds(row, share), :] += jnp.where(col >= left_edge, rows, 0.0)
            total[pl.ds(row + strip, share), :] += jnp.where(col < left_edge, rows, 0.0)

    for h in range(2):
        repeat(slots, peers, lambda b, h=h: place_rows(h, b))
    for j in range(tiles):
        tile = pl.ds((sky ^ j) * size, size)
        value = sums[0][tile, :]
        for total in sums[1:]:
            value = value + total[tile, :]
        pieces[j][pl.ds(0, size), :] = value
        pieces[j][pl.ds(size, meta_rows), :] = meta


def template_kernel(tiles, strip, visits, meta_blocks, side, *refs):
    sources, out = refs[:tiles], refs[tiles]
    visit = lax.axis_index("visit")
    sky = lax.axis_index("sky")
    size = 2 * strip
    value = sources[0][...]
    for p in range(1, tiles):
        value = value + sources[p][...]
    y = (lax.broadcasted_iota(jnp.int32, (strip, LANES), 0) * visits + visit).astype(F32)
    x = lax.broadcasted_iota(jnp.int32, (TILE, LANES), 0).astype(F32)
    coverage = jnp.zeros((strip, TILE), F32)
    for m in range(meta_blocks):
        meta = value[size + m * META : size + (m + 1) * META]
        used, top, left, owner = meta[0:1], meta[1:2], meta[2:3], meta[3:4]
        inside = (y >= top) & (y < top + side) & (owner == sky.astype(F32))
        amount = jnp.where(inside, jnp.broadcast_to(used, y.shape), 0.0)
        columns = jnp.where((x >= left) & (x < left + side), 1.0, 0.0).astype(BF16)
        one, _ = split(amount)
        two = (amount - one.astype(F32)).astype(BF16)
        three = (amount - one.astype(F32) - two.astype(F32)).astype(BF16)
        for part in (one, two, three):
            coverage = coverage + lax.dot_general(
                part, columns, (((1,), (1,)), ((), ())), preferred_element_type=F32
            )
    for h in range(2):
        out[pl.ds(h * strip, strip), :] = value[h * strip : (h + 1) * strip] / (
            coverage[:, h * LANES : (h + 1) * LANES] + 1.0
        )


def hold_kernel(source, out):
    out[...] = source[pl.ds(0, META), :]


def select_kernel(slots, side, tiles, visits, scalars, *refs):
    peers = visits // 2
    share = side // visits
    strip = TILE // visits
    sources, pieces, tile_rows = refs[:tiles], refs[tiles : tiles + peers], refs[tiles + peers]
    visit = lax.axis_index("visit")
    sky = lax.axis_index("sky")
    core = visit % 2
    place = visit // 2
    for j in range(tiles):
        tile_rows[pl.ds((sky ^ j) * 2 * strip, 2 * strip), :] = sources[j][...]
    col = lax.broadcasted_iota(jnp.int32, (share, LANES), 1)
    for j in range(peers):
        piece = pieces[j]
        piece[pl.ds(2 * slots * share, 2 * strip), :] = sources[0][...]

        def pick(n, j=j, piece=piece):
            h, b = quotient(n, slots), n % slots
            reader = 2 * (place ^ j) + (core ^ h)
            row, left_edge = look_up(scalars, (reader * tiles + sky) * slots + b)
            piece[pl.ds(n * share, share), :] = jnp.where(
                col >= left_edge,
                tile_rows[pl.ds(row, share), :],
                tile_rows[pl.ds(row + strip, share), :],
            )

        repeat(2 * slots, peers, pick)


def second_kernel(
    slots, side, strip, peers,
    left, across_high, across_low, science, counts, places,
    *refs,
):
    pieces, refs = refs[: 2 * peers], refs[2 * peers :]
    template, difference, images, right, total, windows, staged, results, outward = refs[-9:]
    visits = 2 * peers
    share = side // visits
    visit = lax.axis_index("visit")
    core = visit % 2
    place = visit // 2
    for c in range(2):
        for j in range(peers):
            residue = 2 * (place ^ j) + (core ^ c)
            piece = pieces[c * peers + j]

            for h in range(2):
                total[h, pl.ds(residue, strip, stride=visits), :] = piece[
                    pl.ds(2 * slots * share + h * strip, strip), :
                ]

            def spread_rows(b, c=c, residue=residue, piece=piece):
                top = places[1, b]
                start = first_row(top, residue, visits) * visits + residue - top
                windows[b, pl.ds(start, share, stride=visits), :] = piece[
                    pl.ds((c * slots + b) * share, share), :
                ]

            repeat(slots, peers, spread_rows)
    for h in range(2):
        staged[:, h * LANES : (h + 1) * LANES] = total[h]
    copies = [pltpu.make_async_copy(staged, template.at[0], outward.at[slots])]
    copies[0].start()
    for b in range(slots):
        block = pltpu.roll(windows[b], (side - places[2, b]) % side, 1)
        put_block(block, b, side, images)
    across_stage(slots, side, images, across_high, across_low, right)
    for b in range(slots):
        matched = down_stage(b, side, left, right)
        results[b] = jnp.where(b < counts[0, 0], science[0, b] - matched, 0.0)
        copies.append(pltpu.make_async_copy(results.at[b], difference.at[0, b], outward.at[b]))
        copies[-1].start()
    for copy in copies:
        copy.wait()


def prepare_kernel(
    slots, side, coef, rows_high, rows_low, slot_tile, offsets, tile_place, *refs,
):
    left, places = refs[3:5]
    coef_buf, tap_buf, semaphores = refs[8:]
    wait, _ = fetch(refs[:3], refs[5:8], semaphores)
    for b in range(slots):
        places[0, b] = tile_place[slot_tile[0, b]]
        places[1, b] = offsets[0, 0, b]
        places[2, b] = offsets[0, 1, b]
    tap_rows(coef, coef_buf, tap_buf, rows_high, rows_low, slots)
    for b in range(slots):
        build_left(b, slots, side, tap_buf, left)
    wait(0, 1, 2)


def body(science, coef_first, coef_second, weight, slot_tile, offsets, counts, tile_place):
    slots, side = science.shape[1], science.shape[2]
    basis = coef_first.shape[-1]
    visits = lax.axis_size("visit")
    tiles = lax.axis_size("sky")
    peers = visits // 2
    strip = TILE // visits
    rows = slots * (side // visits)
    meta_blocks = -(-visits * tiles * slots // LANES)
    meta_rows = meta_blocks * META
    across_high, across_low, rows_high, rows_low = (
        jnp.asarray(c) for c in constants(side, basis)
    )
    vmem = pl.BlockSpec(memory_space=pltpu.VMEM)
    smem = pl.BlockSpec(memory_space=pltpu.SMEM)
    anywhere = pl.BlockSpec(memory_space=pl.ANY)

    coef_first = coef_first.transpose(0, 2, 1, 3)
    coef_second = coef_second.transpose(0, 2, 1, 3)
    offsets = offsets.transpose(0, 2, 1)

    def shape(*dims):
        return pltpu.VMEM(dims, F32)

    def far(value):
        return pltpu.with_memory_space_constraint(value, pltpu.HBM)

    def near(value):
        return pltpu.with_memory_space_constraint(value, pltpu.VMEM)

    def call(function, ins, outs, specs=None, scratch=(), out_space=vmem):
        return pl.pallas_call(
            function,
            out_shape=outs,
            in_specs=specs or [vmem] * len(ins),
            out_specs=out_space
            if isinstance(out_space, list)
            else jax.tree.map(lambda _: out_space, outs),
            scratch_shapes=list(scratch),
            compiler_params=pltpu.CompilerParams(vmem_limit_bytes=VMEM_BYTES),
        )(*ins)

    tap_scratch = [
        pltpu.VMEM((-(-3 * row_pitch(slots) // 16) * 16, LANES), F32),
        pltpu.VMEM((-(-3 * row_pitch(slots) // 16) * 16, PROFILES * side), F32),
    ]
    left_shape = (slots, 4 * side, PROFILES * side)
    pass_scratch = [
        pltpu.VMEM((slots * side, 2 * side), BF16),
        pltpu.VMEM((slots, PROFILES * side, 2 * side), BF16),
        pltpu.VMEM((2, TILE, LANES), F32),
        pltpu.VMEM((slots, side, LANES), F32),
    ]

    def flip(value, axis, size, mask):
        return lax.ppermute(value, axis, [(d, d ^ mask) for d in range(size)])

    def exchange(values, axis, size, step):
        out = [values[0]]
        for j in range(1, len(values)):
            out.append(flip(values[j], axis, size, step * j))
        return out

    first_far = (
        coef_first, rows_high, rows_low, science, across_high, across_low,
        weight, slot_tile, offsets, tile_place,
    )
    keep, send = call(
        lambda *refs: first_kernel(slots, side, tiles, meta_blocks, visits, *refs),
        (*map(far, first_far), counts),
        [shape(peers * rows + meta_rows, LANES)] * 2,
        specs=[anywhere] * FIRST_FAR + [smem],
        scratch=tap_scratch
        + [pltpu.VMEM(left_shape, BF16)]
        + pass_scratch[:2]
        + [pltpu.VMEM((slots, side, LANES), F32)]
        + [pltpu.VMEM(a.shape, a.dtype) for a in first_far[:6]]
        + [pltpu.SMEM(a.shape, a.dtype) for a in first_far[6:]]
        + [pltpu.SemaphoreType.DMA((FIRST_FAR,))],
    )
    ready = (across_high, across_low, science)
    left, places, *ready = call(
        lambda *refs: prepare_kernel(slots, side, *refs),
        tuple(
            map(far, (coef_second, rows_high, rows_low, slot_tile, offsets, tile_place, *ready))
        ),
        [pltpu.VMEM(left_shape, BF16), pltpu.SMEM((3, slots), jnp.int32)]
        + [pltpu.VMEM(a.shape, a.dtype) for a in ready],
        specs=[vmem] * 3 + [smem] * 3 + [anywhere] * 3,
        scratch=tap_scratch + [pltpu.SemaphoreType.DMA((3,))],
        out_space=[vmem, smem] + [vmem] * 3,
    )
    received = flip(send, "visit", visits, 1)
    pieces = call(
        lambda *refs: scatter_kernel(rows, peers, meta_rows, *refs),
        (near(keep), near(received)),
        [shape(2 * rows + meta_rows, LANES)] * peers,
    )
    arrived = exchange(pieces, "visit", visits, 2)
    *pieces, scalars = call(
        lambda *refs: plane_kernel(slots, side, tiles, visits, meta_rows, *refs),
        [near(a) for a in arrived],
        [shape(2 * strip + meta_rows, LANES)] * tiles + [pltpu.SMEM((meta_rows, LANES), jnp.int32)],
        out_space=[vmem] * tiles + [smem],
        scratch=[pltpu.VMEM((meta_rows, LANES), jnp.int32), pltpu.SemaphoreType.DMA]
        + [pltpu.VMEM((tiles * 2 * strip, LANES), F32)] * min(peers, 4),
    )
    arrived = exchange(pieces, "sky", tiles, 1)
    strip_own = call(
        lambda *refs: template_kernel(tiles, strip, visits, meta_blocks, side, *refs),
        [near(a) for a in arrived],
        shape(2 * strip, LANES),
    )
    strips = exchange([strip_own] * tiles, "sky", tiles, 1)
    pieces = call(
        lambda *refs: select_kernel(slots, side, tiles, visits, *refs),
        (pltpu.with_memory_space_constraint(scalars, pltpu.SMEM), *map(near, strips)),
        [shape(2 * strip + 2 * rows, LANES)] * peers,
        specs=[smem] + [vmem] * tiles,
        scratch=[pltpu.VMEM((tiles * 2 * strip, LANES), F32)],
    )
    mine = exchange(pieces, "visit", visits, 2)
    theirs, markers = [], []
    for j in range(peers):
        theirs.append(flip(mine[j], "visit", visits, 1))
        if j > 1:
            markers.append(call(hold_kernel, (near(mine[j]),), shape(META, LANES)))
    template, difference = call(
        lambda *refs: second_kernel(slots, side, strip, peers, *refs),
        (near(left), *map(near, ready), counts,
         pltpu.with_memory_space_constraint(places, pltpu.SMEM),
         *map(near, mine), *map(near, theirs), *map(near, markers)),
        [jax.ShapeDtypeStruct(d, F32) for d in ((1, TILE, TILE), (1, slots, side, side))],
        specs=[vmem] * 4 + [smem] * 2 + [vmem] * (2 * peers + len(markers)),
        scratch=pass_scratch
        + [pltpu.VMEM((TILE, TILE), F32), pltpu.VMEM((slots, side, side), F32)]
        + [pltpu.SemaphoreType.DMA((slots + 1,))],
        out_space=anywhere,
    )
    return template, difference


def solution(mesh):
    in_specs = (
        P("visit", "sky", None, None),
        P("visit", "sky", None, None),
        P("visit", "sky", None, None),
        P("visit", "sky"),
        P("visit", "sky"),
        P("visit", "sky", None),
        P("visit", "sky"),
        P(),
    )
    out_specs = (P("sky", None, None), P("visit", "sky", None, None))

    return jax.shard_map(body, mesh=mesh, in_specs=in_specs, out_specs=out_specs, check_vma=False)
```
